512 devices in a mesh: member: 32 (over y, z_lo, core), region: 16 (over z_hi, x).
Axes of the slice: x: 4, y: 4, z: 16 (z_hi: 4, z_lo: 4; z = z_hi * 4 + z_lo), core: 2. Of those that a mesh axis runs over, the one named last changes fastest.
Arguments:
- ensemble: float32 [256, 76, 8192], P('member', None, 'region'), may hold values from -6 to 6
- blending_matrix: float32 [76, 76], replicated, may hold values from -0.625 to 0.625
- lateral_spreading: float32 [76], replicated, may hold values from 0.19 to 0.2
- obs_op: float32 [1024, 128, 608], P(('region', 'member')), may hold values from -0.25 to 0.25
- obs_value: float32 [1024, 128], P(('region', 'member')), may hold values from -6 to 6
- obs_precision: float32 [1024, 128], P(('region', 'member')), may hold values from 0.01 to 3000
Outputs:
- analysis: float32 [256, 76, 8192], P('member', None, 'region')
The draws below stay inside these ranges and needn't reach their ends.
All inputs are finite; a program needn't handle non-finite values.
Results may differ from the reference program's by a relative error of at most 0.0003.
Values sent between devices are 32-bit elements; how exact they have to be, the bound alone decides.
No kernel may reach another device: no remote copies, remote signals or barrier semaphores. Data moves between devices by JAX's collectives and lax.ppermute only.
A program may use at most 64 MiB of HBM per device.

```python
import math
from functools import partial
import jax
import jax.numpy as jnp
from jax import lax

ENSEMBLE_SIZE = 256
LAYER_SUM = 76
GY = 128
TILE_WIDTH = 8
NOBS = 128
NSTEP = 4
ITERS = 12
GX = 64
COLS = 8192
TILE_NUMBER = 1024
S = 608


def draw_obs_precision(key, part):
    fraction = jax.random.uniform(key, (TILE_NUMBER, NOBS), jnp.float32)
    lowest = -4.605170186
    spread_log = 12.611537754
    values = jnp.exp(lowest + fraction * spread_log)
    return jnp.clip(values, 0.01, 3000.0).astype(jnp.float32)


def block_scale(rng, shape, pieces, smallest, largest):
    factor_of, own = 1.0, jax.random.fold_in(rng, 6)
    for dim, shards_of in pieces:
        steps = jnp.exp(jax.random.uniform(jax.random.fold_in(own, dim), (shards_of,), jnp.float32, smallest / len(pieces), largest / len(pieces)))
        factor_of = factor_of * jnp.repeat(steps, shape[dim] // shards_of).reshape([-1 if axis == dim else 1 for axis in range(len(shape))])
    return factor_of


def scatter_about(own_key, shape, deviation, bound, cuts=(), held_as=jnp.bfloat16):
    gain = block_scale(own_key, shape, cuts, -0.22, 0.18) if cuts else 1.0
    array = jax.random.normal(own_key, shape, jnp.float32) * deviation * gain
    return jnp.minimum(jnp.maximum(array, -bound), bound).astype(held_as)


def setup_inputs(seed: int = 0) -> dict:
    keys = jax.random.split(jax.random.key(seed), 7)
    ensemble = scatter_about(keys[0], (ENSEMBLE_SIZE, LAYER_SUM, COLS), 1.0, 6.0, ((0, 32), (2, 16)), jnp.float32)
    blending_matrix = scatter_about(keys[1], (LAYER_SUM, LAYER_SUM), LAYER_SUM ** -0.5, 0.625, (), jnp.float32)
    lateral_spreading = jnp.clip(jax.random.uniform(keys[2], (LAYER_SUM,), jnp.float32, 0.19, 0.2), 0.19, 0.2)
    obs_op = scatter_about(keys[3], (TILE_NUMBER, NOBS, S), S ** -0.5, 0.25, ((0, 512),), jnp.float32)
    obs_value = scatter_about(keys[4], (TILE_NUMBER, NOBS), 1.0, 6.0, ((0, 512),), jnp.float32)
    obs_precision = draw_obs_precision(jax.random.fold_in(keys[6], 71), 0)
    return dict(ensemble=ensemble, blending_matrix=blending_matrix, lateral_spreading=lateral_spreading, obs_op=obs_op, obs_value=obs_value, obs_precision=obs_precision)


HIGHEST = lax.Precision.HIGHEST

def realisation_prediction(layered_variables, blending_matrix, lateral_spreading):
    for step_index in range(NSTEP):
        laplace = jnp.roll(layered_variables, -1, 1) + jnp.roll(layered_variables, 1, 1) + jnp.roll(layered_variables, -1, 2) + jnp.roll(layered_variables, 1, 2) - 4.0 * layered_variables
        coupled = jnp.einsum('fg,gxy->fxy', blending_matrix, layered_variables, precision=HIGHEST)
        layered_variables = layered_variables + lateral_spreading[:, None, None] * laplace + 0.3 * jnp.tanh(coupled)
    return layered_variables

def analyse(packed):
    patch_state, operator, observed, precisions = packed
    mean_state = lax.optimization_barrier(jnp.mean(patch_state, axis=0))
    perturb = patch_state - mean_state
    obs_pert = jnp.dot(perturb, operator.T, precision=HIGHEST, preferred_element_type=jnp.float32)
    obs_mean = jnp.dot(operator, mean_state, precision=HIGHEST, preferred_element_type=jnp.float32)
    innovation = observed - obs_mean
    weighted = obs_pert * precisions
    gram_matrix = jnp.dot(weighted, obs_pert.T, precision=HIGHEST, preferred_element_type=jnp.float32)
    identity = jnp.eye(ENSEMBLE_SIZE, dtype=jnp.float32)
    system = (ENSEMBLE_SIZE - 1.0) * identity + gram_matrix
    norm_scale = jnp.sqrt(jnp.sum(system * system))
    sqrt_iter = system / norm_scale
    inv_iter = identity
    for step_index in range(ITERS):
        factor = 0.5 * (3.0 * identity - jnp.dot(inv_iter, sqrt_iter, precision=HIGHEST, preferred_element_type=jnp.float32))
        sqrt_iter = jnp.dot(sqrt_iter, factor, precision=HIGHEST, preferred_element_type=jnp.float32)
        inv_iter = jnp.dot(factor, inv_iter, precision=HIGHEST, preferred_element_type=jnp.float32)
    inv_sqrt = inv_iter / jnp.sqrt(norm_scale)
    inverse = jnp.dot(inv_sqrt, inv_sqrt, precision=HIGHEST, preferred_element_type=jnp.float32)
    mean_w = jnp.dot(inverse, jnp.dot(weighted, innovation, precision=HIGHEST, preferred_element_type=jnp.float32), precision=HIGHEST, preferred_element_type=jnp.float32)
    weights = math.sqrt(ENSEMBLE_SIZE - 1.0) * inv_sqrt + mean_w[:, None]
    return mean_state + jnp.dot(weights.T, perturb, precision=HIGHEST, preferred_element_type=jnp.float32)

def reference(ensemble, blending_matrix, lateral_spreading, obs_op, obs_value, obs_precision):
    realisation_lattice = ensemble.reshape(ENSEMBLE_SIZE, LAYER_SUM, GX, GY)
    predict_advance = lax.map(partial(realisation_prediction, blending_matrix=blending_matrix, lateral_spreading=lateral_spreading), realisation_lattice)
    neighbourhood_tiles = predict_advance.reshape(ENSEMBLE_SIZE, LAYER_SUM, TILE_NUMBER, TILE_WIDTH).transpose(2, 0, 1, 3).reshape(TILE_NUMBER, ENSEMBLE_SIZE, LAYER_SUM * TILE_WIDTH)
    result = lax.map(analyse, (neighbourhood_tiles, obs_op, obs_value, obs_precision))
    return result.reshape(TILE_NUMBER, ENSEMBLE_SIZE, LAYER_SUM, TILE_WIDTH).transpose(1, 2, 0, 3).reshape(ENSEMBLE_SIZE, LAYER_SUM, COLS)
```

```python
import math

import jax
import jax.numpy as jnp
from jax import lax
from jax.experimental import pallas as pl
from jax.experimental.pallas import tpu as pltpu
from jax.sharding import Mesh, PartitionSpec as P

F32 = jnp.float32
BF16 = jnp.bfloat16
HIGHEST = lax.Precision.HIGHEST
LEVELS = 76
PADDED = 80
GY = 128
NSTEP = 4
ITERS = 12
MEMBERS = 256
PAIR = 2 * LEVELS * 16
TILES = PAIR // 128
HALF = LEVELS * 16
LANES = 1280
VMEM_LIMIT = 32 * 1024 * 1024


def lane_index(shape):
    return lax.broadcasted_iota(jnp.int32, shape, len(shape) - 1)


def split3(x):
    high = x.astype(BF16)
    rest = x - high.astype(F32)
    mid = rest.astype(BF16)
    low = (rest - mid.astype(F32)).astype(BF16)
    return high, mid, low


def swap_blocks(x):
    sub = lax.broadcasted_iota(jnp.int32, x.shape, 1)
    block = lane_index(x.shape) // 16
    for bit in (1, 2, 4):
        up = (sub & bit) != 0
        keep = up == ((block & bit) != 0)
        lanes = 16 * bit
        lower = pltpu.roll(pltpu.roll(x, 8 - bit, 1), lanes, 2)
        if bit == 4:
            other = lower
        else:
            upper = pltpu.roll(pltpu.roll(x, bit, 1), 128 - lanes, 2)
            other = jnp.where(up, upper, lower)
        x = jnp.where(keep, x, other)
    return x


def forecast_kernel(main_ref, prev_ref, next_ref, mix_ref, rate_ref, out_ref, state, mix, rate):
    wide = mix_ref[...]
    high, mid, low = split3(wide)
    part = lane_index(wide.shape) // PADDED
    pick_mid = (part == 2) | (part == 3)
    mix[...] = jnp.where(
        pick_mid, mid.astype(F32), jnp.where(part == 5, low.astype(F32), high.astype(F32))
    ).astype(BF16)
    rate[...] = jnp.broadcast_to(rate_ref[...], (PADDED, GY))
    pad = jnp.zeros((PADDED - LEVELS, GY), F32)
    for m in range(2):
        for row in range(24):
            cols = pl.ds((row % 4) * GY, GY)
            if row < 4:
                cells = prev_ref[m, :, cols]
            elif row < 20:
                cells = main_ref[row // 4 - 1, m, :, cols]
            else:
                cells = next_ref[m, :, cols]
            state[0, m, row, 0:LEVELS, :] = cells
            state[0, m, row, LEVELS:PADDED, :] = pad

    def advance(now, m, row):
        centre = [state[now, m, row + i] for i in range(2)]
        before = state[now, m, row - 1]
        after = state[now, m, row + 2]
        parts = split3(jnp.concatenate(centre, axis=1))
        stacked = jnp.concatenate([parts[i] for i in (0, 1, 0, 1, 2, 0)], axis=0)
        coupled = jnp.dot(mix[...], stacked, preferred_element_type=F32)
        result = []
        for i in range(2):
            cells = centre[i]
            around = (centre[1] + before) if i == 0 else (after + centre[0])
            laplace = (
                around + pltpu.roll(cells, GY - 1, 1) + pltpu.roll(cells, 1, 1) - 4.0 * cells
            )
            pushed = jnp.tanh(coupled[:, i * GY : (i + 1) * GY])
            result.append(cells + rate[...] * laplace + 0.3 * pushed)
        return result

    for step in range(NSTEP - 1):
        now = step % 2

        def body(pair, carry, now=now, step=step):
            row = step + 1 + 2 * pair
            for m in range(2):
                result = advance(now, m, row)
                state[1 - now, m, row] = result[0]
                state[1 - now, m, row + 1] = result[1]
            return carry

        lax.fori_loop(0, (22 - 2 * step) // 2, body, 0)

    def last(pair, carry):
        row = 4 + 2 * pair
        results = [advance((NSTEP - 1) % 2, m, row) for m in range(2)]
        for i in range(2):
            both = jnp.concatenate([results[m][i][0:LEVELS] for m in range(2)], axis=0)
            moved = swap_blocks(both.reshape(TILES, 8, GY))
            start = (2 * pair + i) * 8
            for tile in range(TILES):
                out_ref[pl.ds(start, 8), 0, pl.ds(tile * 128, 128)] = moved[tile]
        return carry

    lax.fori_loop(0, 8, last, 0)


def analysis_kernel(x_ref, op_ref, obs_ref, prec_ref, out_ref, pert, wide, yref, rr, zz, ff, moved):
    low_half = lane_index((128, 128)) < 64
    rows = 128
    for tile in range(10):
        even = x_ref[:, 0, pl.ds(tile * 128, 128)]
        first = x_ref[:, 0, pl.ds((9 + tile) * 128, 128)]
        if tile < 9:
            second = x_ref[:, 0, pl.ds((10 + tile) * 128, 128)]
            odd = pltpu.roll(jnp.where(low_half, second, first), 64, 1)
        else:
            even = jnp.where(low_half, even, 0.0)
            odd = jnp.where(low_half, pltpu.roll(first, 64, 1), 0.0)
        mean = (jnp.sum(even, axis=0, keepdims=True) + jnp.sum(odd, axis=0, keepdims=True)) / MEMBERS
        lanes = pl.ds(tile * 128, 128)
        pert[0:rows, lanes] = even - mean
        pert[rows : 2 * rows, lanes] = odd - mean
        pert[2 * rows : 2 * rows + 8, lanes] = jnp.broadcast_to(mean, (8, 128))

    take = lax.broadcasted_iota(jnp.int32, (128, 256), 0)
    put = lane_index((128, 256))
    same = (put // 16 == take // 8) & (put % 8 == take % 8)
    spread = jnp.where(same, 1.0, 0.0).astype(BF16)
    group = (lane_index((128, 256)) // 8) % 2
    for j in range(2):
        for block in range(5):
            width = 128 if block < 4 else 608 - 512
            piece = split3(op_ref[j, :, pl.ds(block * 128, width)])
            grown = [
                jnp.dot(p, spread[0:width], preferred_element_type=F32) for p in piece
            ]
            full = (grown[0] + grown[1]) + grown[2]
            wide[j * 128 : (j + 1) * 128, block * 256 : (block + 1) * 256] = jnp.where(
                group == j, full, 0.0
            )

    yref[...] = lax.dot_general(
        pert[...], wide[...], (((1,), (1,)), ((), ())), precision=HIGHEST, preferred_element_type=F32
    )
    eye = jnp.where(
        lax.broadcasted_iota(jnp.int32, (MEMBERS, MEMBERS), 0) == lane_index((MEMBERS, MEMBERS)), 1.0, 0.0
    )

    def mm(a, b):
        return jnp.dot(a, b, precision=HIGHEST, preferred_element_type=F32)

    scale = []
    for j in range(2):
        obs = slice(j * 128, (j + 1) * 128)
        y = yref[0:MEMBERS, obs]
        weighted = y * prec_ref[j : j + 1, :]
        gram = lax.dot_general(
            weighted, y, (((1,), (1,)), ((), ())), precision=HIGHEST, preferred_element_type=F32
        )
        system = (MEMBERS - 1.0) * eye + gram
        norm = jnp.sqrt(jnp.sum(jnp.sum(system * system, axis=0, keepdims=True), axis=1, keepdims=True))
        scale.append(norm)
        start = system / norm
        factor = 0.5 * (3.0 * eye - start)
        ff[j] = start
        zz[j] = factor
        rr[j] = mm(start, factor)

    def body(step, carry):
        for j in range(2):
            ff[j] = 0.5 * (3.0 * eye - mm(zz[j], rr[j]))
        for j in range(2):
            rr[j] = mm(rr[j], ff[j])
        for j in range(2):
            zz[j] = mm(ff[j], zz[j])
        return carry

    lax.fori_loop(0, ITERS - 2, body, 0)
    shifts = []
    for j in range(2):
        factor = 0.5 * (3.0 * eye - mm(zz[j], rr[j]))
        root = mm(factor, zz[j]) / jnp.sqrt(scale[j])
        obs = slice(j * 128, (j + 1) * 128)
        y = yref[0:MEMBERS, obs]
        innovation = obs_ref[j : j + 1, :] - yref[MEMBERS : MEMBERS + 1, obs]
        pull = jnp.sum(y * prec_ref[j : j + 1, :] * innovation, axis=1, keepdims=True)
        half = jnp.sum(root * pull, axis=0, keepdims=True)
        weight = jnp.sum(root * half, axis=1, keepdims=True)
        zz[j] = math.sqrt(MEMBERS - 1.0) * root
        shifts.append(weight)
    for block in range(5):
        lanes = pl.ds(block * 256, 256)
        own = (lane_index((MEMBERS, 256)) // 8) % 2 == 0
        cells = pert[0:MEMBERS, lanes]
        terms = []
        for j in range(2):
            base = pert[MEMBERS : MEMBERS + 1, lanes] + jnp.sum(cells * shifts[j], axis=0, keepdims=True)
            terms.append(base + mm(zz[j], cells))
        moved[:, lanes] = jnp.where(own, terms[0], terms[1])
    for tile in range(TILES):
        if tile < 9:
            value = moved[0:rows, tile * 128 : (tile + 1) * 128]
        elif tile == 9:
            rolled = pltpu.roll(moved[rows : 2 * rows, 0:128], 64, 1)
            value = jnp.where(low_half, moved[0:rows, 9 * 128 : 10 * 128], rolled)
        else:
            i = tile - 10
            first = moved[rows : 2 * rows, i * 128 : (i + 1) * 128]
            second = moved[rows : 2 * rows, (i + 1) * 128 : (i + 2) * 128]
            value = pltpu.roll(jnp.where(low_half, second, first), 64, 1)
        for s in range(4):
            out_ref[:, 0, pl.ds(s * PAIR + tile * 128, 128)] = value[s * 32 : (s + 1) * 32]


def restore_kernel(in_ref, out_ref):
    def body(s, carry):
        for y in range(4):
            tiles = [
                in_ref[pl.ds(y * 8, 8), 0, pl.ds(pl.multiple_of(s * PAIR + tile * 128, 128), 128)]
                for tile in range(TILES)
            ]
            moved = swap_blocks(jnp.stack(tiles, axis=0)).reshape(2 * LEVELS, GY)
            out_ref[2 * s, :, y * GY : (y + 1) * GY] = moved[0:LEVELS]
            out_ref[2 * s + 1, :, y * GY : (y + 1) * GY] = moved[LEVELS : 2 * LEVELS]
        return carry

    lax.fori_loop(0, 4, body, 0)


def params():
    return pltpu.CompilerParams(vmem_limit_bytes=VMEM_LIMIT)


def forecast(main, before, after, mixing, rate):
    return pl.pallas_call(
        forecast_kernel,
        out_shape=jax.ShapeDtypeStruct((128, 1, PAIR), F32),
        scratch_shapes=[
            pltpu.VMEM((2, 2, 24, PADDED, GY), F32),
            pltpu.VMEM((PADDED, 6 * PADDED), BF16),
            pltpu.VMEM((PADDED, GY), F32),
        ],
        compiler_params=params(),
        name="forecast",
    )(main, before, after, mixing, rate)


def analyse(cells, operator, observed, precisions):
    return pl.pallas_call(
        analysis_kernel,
        out_shape=jax.ShapeDtypeStruct((32, 1, 4 * PAIR), F32),
        scratch_shapes=[
            pltpu.VMEM((MEMBERS + 8, LANES), F32),
            pltpu.VMEM((2 * 128, LANES), F32),
            pltpu.VMEM((MEMBERS + 8, 2 * 128), F32),
            pltpu.VMEM((2, MEMBERS, MEMBERS), F32),
            pltpu.VMEM((2, MEMBERS, MEMBERS), F32),
            pltpu.VMEM((2, MEMBERS, MEMBERS), F32),
            pltpu.VMEM((MEMBERS, LANES), F32),
        ],
        compiler_params=params(),
        name="analysis",
    )(cells, operator, observed, precisions)


def restore(cells):
    return pl.pallas_call(
        restore_kernel,
        out_shape=jax.ShapeDtypeStruct((8, LEVELS, 4 * GY), F32),
        compiler_params=params(),
        name="restore",
    )(cells)


def prepare(blending_matrix, lateral_spreading):
    extra = PADDED - LEVELS
    mixing = jnp.tile(jnp.pad(blending_matrix, ((0, extra), (0, extra))), (1, 6))
    return mixing, jnp.pad(lateral_spreading, (0, extra))[:, None]


def shards(ensemble, blending_matrix, lateral_spreading, obs_op, obs_value, obs_precision):
    mixing, rate = prepare(blending_matrix, lateral_spreading)
    split = ensemble.reshape(4, 2, LEVELS, 4 * GY)
    main = lax.all_to_all(split, "x", split_axis=0, concat_axis=0, tiled=True)
    before = lax.ppermute(main[3], "zh", [(i, (i + 1) % 4) for i in range(4)])
    after = lax.ppermute(main[0], "zh", [((i + 1) % 4, i) for i in range(4)])
    sent = forecast(main, before, after, mixing, rate)
    owned = lax.all_to_all(sent, ("x", "y", "zl", "c"), split_axis=0, concat_axis=0, tiled=True)
    result = analyse(owned, obs_op, obs_value, obs_precision)
    returned = lax.all_to_all(result, ("y", "zl", "c"), split_axis=0, concat_axis=0, tiled=True)
    return restore(returned)


def solution(mesh):
    fine = Mesh(mesh.devices.reshape(4, 4, 2, 4, 4), ("y", "zl", "c", "zh", "x"))
    member, region = ("y", "zl", "c"), ("zh", "x")
    return jax.shard_map(
        shards,
        mesh=fine,
        in_specs=(
            P(member, None, region),
            P(),
            P(),
            P(region + member, None, None),
            P(region + member, None),
            P(region + member, None),
        ),
        out_specs=P(member, None, region),
        check_vma=False,
    )
```

```python
import math

import jax
import jax.numpy as jnp
from jax import lax
from jax.experimental import pallas as pl
from jax.experimental.pallas import tpu as pltpu
from jax.sharding import Mesh, PartitionSpec as P

F32 = jnp.float32
BF16 = jnp.bfloat16
HIGHEST = lax.Precision.HIGHEST
LEVELS = 76
PADDED = 80
GY = 128
NSTEP = 4
ITERS = 12
MEMBERS = 256
BLOCKS = 5
WIDTH = BLOCKS * 128
CHUNK = 2 * WIDTH
VMEM_LIMIT = 32 * 1024 * 1024


def lane_index(shape):
    return lax.broadcasted_iota(jnp.int32, shape, len(shape) - 1)


def split3(x):
    high = x.astype(BF16)
    rest = x - high.astype(F32)
    mid = rest.astype(BF16)
    low = (rest - mid.astype(F32)).astype(BF16)
    return high, mid, low


def swap_blocks(x):
    sub = lax.broadcasted_iota(jnp.int32, x.shape, 1)
    block = lane_index(x.shape) // 16
    for bit in (1, 2, 4):
        up = (sub & bit) != 0
        keep = up == ((block & bit) != 0)
        lanes = 16 * bit
        lower = pltpu.roll(pltpu.roll(x, 8 - bit, 1), lanes, 2)
        if bit == 4:
            other = lower
        else:
            upper = pltpu.roll(pltpu.roll(x, bit, 1), 128 - lanes, 2)
            other = jnp.where(up, upper, lower)
        x = jnp.where(keep, x, other)
    return x


def forecast_kernel(main_ref, prev_ref, next_ref, mix_ref, rate_ref, out0_ref, out1_ref, state, mix, rate):
    wide = mix_ref[...]
    high, mid, low = split3(wide)
    part = lane_index(wide.shape) // PADDED
    pick_mid = (part == 2) | (part == 3)
    mix[...] = jnp.where(
        pick_mid, mid.astype(F32), jnp.where(part == 5, low.astype(F32), high.astype(F32))
    ).astype(BF16)
    rate[...] = jnp.broadcast_to(rate_ref[...], (PADDED, GY))
    pad = jnp.zeros((PADDED - LEVELS, GY), F32)
    for m in range(2):
        for row in range(24):
            cols = pl.ds((row % 4) * GY, GY)
            if row < 4:
                cells = prev_ref[m, :, cols]
            elif row < 20:
                cells = main_ref[row // 4 - 1, m, :, cols]
            else:
                cells = next_ref[m, :, cols]
            state[0, m, row, 0:LEVELS, :] = cells
            state[0, m, row, LEVELS:PADDED, :] = pad

    def advance(now, m, row):
        centre = [state[now, m, row + i] for i in range(2)]
        before = state[now, m, row - 1]
        after = state[now, m, row + 2]
        parts = split3(jnp.concatenate(centre, axis=1))
        stacked = jnp.concatenate([parts[i] for i in (0, 1, 0, 1, 2, 0)], axis=0)
        coupled = jnp.dot(mix[...], stacked, preferred_element_type=F32)
        result = []
        for i in range(2):
            cells = centre[i]
            around = (centre[1] + before) if i == 0 else (after + centre[0])
            laplace = (
                around + pltpu.roll(cells, GY - 1, 1) + pltpu.roll(cells, 1, 1) - 4.0 * cells
            )
            pushed = jnp.tanh(coupled[:, i * GY : (i + 1) * GY])
            result.append(cells + rate[...] * laplace + 0.3 * pushed)
        return result

    for step in range(NSTEP - 1):
        now = step % 2

        def body(pair, carry, now=now, step=step):
            row = step + 1 + 2 * pair
            for m in range(2):
                result = advance(now, m, row)
                state[1 - now, m, row] = result[0]
                state[1 - now, m, row + 1] = result[1]
            return carry

        lax.fori_loop(0, (22 - 2 * step) // 2, body, 0)

    second = (lane_index((8, GY)) // 8) % 2 == 1

    def last(pair, carry):
        row = 4 + 2 * pair
        for m in range(2):
            result = advance((NSTEP - 1) % 2, m, row)
            for i in range(2):
                start = (2 * pair + i) * 8
                low = result[i].reshape(BLOCKS, 2, 8, GY)
                for j, out_ref in enumerate((out0_ref, out1_ref)):
                    tiles = []
                    for k in range(BLOCKS):
                        if j == 0:
                            tiles.append(jnp.where(second, pltpu.roll(low[k, 1], 8, 1), low[k, 0]))
                        else:
                            tiles.append(jnp.where(second, low[k, 1], pltpu.roll(low[k, 0], GY - 8, 1)))
                    moved = swap_blocks(jnp.stack(tiles, axis=0))
                    for k in range(BLOCKS):
                        out_ref[pl.ds(start, 8), 0, pl.ds(m * WIDTH + k * 128, 128)] = moved[k]
        return carry

    lax.fori_loop(0, 8, last, 0)


def analysis_kernel(x_ref, op_ref, obs_ref, prec_ref, out_ref, pert, wide, yref, rr, zz, ff):
    rows = 128
    take = lax.broadcasted_iota(jnp.int32, (128, 128), 0)
    put = lane_index((128, 128))
    source = ((put // 8) % 2) * 64 + (put // 16) * 8 + put % 8
    order = jnp.where(take == source, 1.0, 0.0).astype(BF16)
    for k in range(BLOCKS):
        lanes = pl.ds(k * 128, 128)
        halves = [x_ref[:, 0, pl.ds(m * WIDTH + k * 128, 128)] for m in range(2)]
        mean = (
            jnp.sum(halves[0], axis=0, keepdims=True) + jnp.sum(halves[1], axis=0, keepdims=True)
        ) / MEMBERS
        for m in range(2):
            pert[m * rows : (m + 1) * rows, lanes] = halves[m] - mean
        pert[MEMBERS : MEMBERS + 8, lanes] = jnp.broadcast_to(mean, (8, 128))
        width = 128 if k < BLOCKS - 1 else 8 * LEVELS - 512
        grown = [
            jnp.dot(p, order[0:width], preferred_element_type=F32)
            for p in split3(op_ref[0, :, pl.ds(k * 128, width)])
        ]
        wide[:, lanes] = (grown[0] + grown[1]) + grown[2]

    yref[...] = lax.dot_general(
        pert[...], wide[...], (((1,), (1,)), ((), ())), precision=HIGHEST, preferred_element_type=F32
    )
    eye = jnp.where(
        lax.broadcasted_iota(jnp.int32, (MEMBERS, MEMBERS), 0) == lane_index((MEMBERS, MEMBERS)), 1.0, 0.0
    )

    def mm(a, b):
        return jnp.dot(a, b, precision=HIGHEST, preferred_element_type=F32)

    y = yref[0:MEMBERS]
    weighted = y * prec_ref[0]
    gram = lax.dot_general(
        weighted, y, (((1,), (1,)), ((), ())), precision=HIGHEST, preferred_element_type=F32
    )
    system = (MEMBERS - 1.0) * eye + gram
    norm = jnp.sqrt(jnp.sum(jnp.sum(system * system, axis=0, keepdims=True), axis=1, keepdims=True))
    start = system / norm
    factor = 0.5 * (3.0 * eye - start)
    zz[...] = factor
    rr[...] = mm(start, factor)

    def body(step, carry):
        ff[...] = 0.5 * (3.0 * eye - mm(zz[...], rr[...]))
        rr[...] = mm(rr[...], ff[...])
        zz[...] = mm(ff[...], zz[...])
        return carry

    lax.fori_loop(0, ITERS - 2, body, 0)
    factor = 0.5 * (3.0 * eye - mm(zz[...], rr[...]))
    root = mm(factor, zz[...]) / jnp.sqrt(norm)
    innovation = obs_ref[0] - yref[MEMBERS : MEMBERS + 1]
    pull = jnp.sum(y * prec_ref[0] * innovation, axis=1, keepdims=True)
    half = jnp.sum(root * pull, axis=0, keepdims=True)
    shift = jnp.sum(root * half, axis=1, keepdims=True)
    zz[...] = math.sqrt(MEMBERS - 1.0) * root
    for start, size in ((0, 256), (256, 256), (512, 128)):
        lanes = pl.ds(start, size)
        cells = pert[0:MEMBERS, lanes]
        base = pert[MEMBERS : MEMBERS + 1, lanes] + jnp.sum(cells * shift, axis=0, keepdims=True)
        moved = base + mm(zz[...], cells)
        for m in range(2):
            for s in range(4):
                first = m * rows + s * 32
                out_ref[:, 0, pl.ds(s * CHUNK + m * WIDTH + start, size)] = moved[first : first + 32]


def restore_kernel(in0_ref, in1_ref, out_ref):
    second = (lane_index((BLOCKS, 8, GY)) // 8) % 2 == 1

    def body(s, carry):
        for m in range(2):
            for y in range(4):
                groups = []
                for in_ref in (in0_ref, in1_ref):
                    tiles = [
                        in_ref[
                            pl.ds(y * 8, 8),
                            0,
                            pl.ds(pl.multiple_of(s * CHUNK + m * WIDTH + k * 128, 128), 128),
                        ]
                        for k in range(BLOCKS)
                    ]
                    groups.append(swap_blocks(jnp.stack(tiles, axis=0)))
                even = jnp.where(second, pltpu.roll(groups[1], 8, 2), groups[0])
                odd = jnp.where(second, groups[1], pltpu.roll(groups[0], GY - 8, 2))
                cols = pl.ds(y * GY, GY)
                for k in range(BLOCKS):
                    out_ref[2 * s + m, pl.ds(16 * k, 8), cols] = even[k]
                    last = 8 if k < BLOCKS - 1 else LEVELS - 72
                    out_ref[2 * s + m, pl.ds(16 * k + 8, last), cols] = odd[k, 0:last]
        return carry

    lax.fori_loop(0, 4, body, 0)


def params():
    return pltpu.CompilerParams(vmem_limit_bytes=VMEM_LIMIT)


def forecast(main, before, after, mixing, rate):
    return pl.pallas_call(
        forecast_kernel,
        out_shape=[jax.ShapeDtypeStruct((128, 1, CHUNK), F32)] * 2,
        scratch_shapes=[
            pltpu.VMEM((2, 2, 24, PADDED, GY), F32),
            pltpu.VMEM((PADDED, 6 * PADDED), BF16),
            pltpu.VMEM((PADDED, GY), F32),
        ],
        compiler_params=params(),
        name="forecast",
    )(main, before, after, mixing, rate)


def analyse(cells, operator, observed, precisions):
    return pl.pallas_call(
        analysis_kernel,
        out_shape=jax.ShapeDtypeStruct((32, 1, 4 * CHUNK), F32),
        scratch_shapes=[
            pltpu.VMEM((MEMBERS + 8, WIDTH), F32),
            pltpu.VMEM((128, WIDTH), F32),
            pltpu.VMEM((MEMBERS + 8, 128), F32),
            pltpu.VMEM((MEMBERS, MEMBERS), F32),
            pltpu.VMEM((MEMBERS, MEMBERS), F32),
            pltpu.VMEM((MEMBERS, MEMBERS), F32),
        ],
        compiler_params=params(),
        cost_estimate=pl.CostEstimate(
            flops=36 * 6 * 2 * MEMBERS**3, bytes_accessed=4 * 2**20, transcendentals=0
        ),
        name="analysis",
    )(cells, operator, observed, precisions)


def restore(first, second):
    return pl.pallas_call(
        restore_kernel,
        out_shape=jax.ShapeDtypeStruct((8, LEVELS, 4 * GY), F32),
        compiler_params=params(),
        name="restore",
    )(first, second)


def prepare(blending_matrix, lateral_spreading):
    extra = PADDED - LEVELS
    mixing = jnp.tile(jnp.pad(blending_matrix, ((0, extra), (0, extra))), (1, 6))
    return mixing, jnp.pad(lateral_spreading, (0, extra))[:, None]


def shards(ensemble, blending_matrix, lateral_spreading, obs_op, obs_value, obs_precision):
    mixing, rate = prepare(blending_matrix, lateral_spreading)
    split = ensemble.reshape(4, 2, LEVELS, 4 * GY)
    main = lax.all_to_all(split, "x", split_axis=0, concat_axis=0, tiled=True)
    before = lax.ppermute(main[3], "zh", [(i, (i + 1) % 4) for i in range(4)])
    after = lax.ppermute(main[0], "zh", [((i + 1) % 4, i) for i in range(4)])
    sent = forecast(main, before, after, mixing, rate)
    owned = [
        lax.all_to_all(part, ("x", "y", "zl", "c"), split_axis=0, concat_axis=0, tiled=True)
        for part in sent
    ]
    returned = []
    for j in range(2):
        result = analyse(
            owned[j], obs_op[j : j + 1], obs_value[j : j + 1, None], obs_precision[j : j + 1, None]
        )
        returned.append(
            lax.all_to_all(result, ("y", "zl", "c"), split_axis=0, concat_axis=0, tiled=True)
        )
    return restore(*returned)


def solution(mesh):
    fine = Mesh(mesh.devices.reshape(4, 4, 2, 4, 4), ("y", "zl", "c", "zh", "x"))
    member, region = ("y", "zl", "c"), ("zh", "x")
    return jax.shard_map(
        shards,
        mesh=fine,
        in_specs=(
            P(member, None, region),
            P(),
            P(),
            P(region + member, None, None),
            P(region + member, None),
            P(region + member, None),
        ),
        out_specs=P(member, None, region),
        check_vma=False,
    )
```

```python
import math

import jax
import jax.numpy as jnp
from jax import lax
from jax.experimental import pallas as pl
from jax.experimental.pallas import tpu as pltpu
from jax.sharding import Mesh, PartitionSpec as P

F32 = jnp.float32
BF16 = jnp.bfloat16
HIGHEST = lax.Precision.HIGHEST
LEVELS = 76
PADDED = 80
GY = 128
NSTEP = 4
ITERS = 12
MEMBERS = 256
PAIR = 2 * LEVELS * 16
TILES = PAIR // 128
HALF = LEVELS * 16
LANES = 1280
VMEM_LIMIT = 32 * 1024 * 1024


def lane_index(shape):
    return lax.broadcasted_iota(jnp.int32, shape, len(shape) - 1)


def split3(x):
    high = x.astype(BF16)
    rest = x - high.astype(F32)
    mid = rest.astype(BF16)
    low = (rest - mid.astype(F32)).astype(BF16)
    return high, mid, low


def swap_blocks(x):
    sub = lax.broadcasted_iota(jnp.int32, x.shape, 1)
    block = lane_index(x.shape) // 16
    for bit in (1, 2, 4):
        up = (sub & bit) != 0
        keep = up == ((block & bit) != 0)
        lanes = 16 * bit
        lower = pltpu.roll(pltpu.roll(x, 8 - bit, 1), lanes, 2)
        if bit == 4:
            other = lower
        else:
            upper = pltpu.roll(pltpu.roll(x, bit, 1), 128 - lanes, 2)
            other = jnp.where(up, upper, lower)
        x = jnp.where(keep, x, other)
    return x


def advance(window, mix_ref, rate_ref):
    centre = window[1:3]
    high, mid, _ = split3(jnp.concatenate(centre, axis=1))
    stacked = jnp.concatenate([high, mid, high], axis=0)
    coupled = jnp.dot(mix_ref[...], stacked, preferred_element_type=F32)
    result = []
    for i in range(2):
        cells = centre[i]
        around = window[i] + window[i + 2]
        laplace = around + pltpu.roll(cells, GY - 1, 1) + pltpu.roll(cells, 1, 1) - 4.0 * cells
        pushed = jnp.tanh(coupled[:, i * GY : (i + 1) * GY])
        result.append(cells + rate_ref[...] * laplace + 0.3 * pushed)
    return result


def send_rows(results, row, out_ref):
    for i in range(2):
        both = jnp.concatenate([results[m][i][0:LEVELS] for m in range(2)], axis=0)
        moved = swap_blocks(both.reshape(TILES, 8, GY))
        for tile in range(TILES):
            out_ref[pl.ds((row + i) * 8, 8), 0, pl.ds(tile * 128, 128)] = moved[tile]


def put_row(state_ref, index, cells):
    state_ref[index + (slice(0, LEVELS), slice(None))] = cells
    state_ref[index + (slice(LEVELS, PADDED), slice(None))] = jnp.zeros((PADDED - LEVELS, GY), F32)


def interior_kernel(main_ref, mix_ref, rate_ref, op_ref, out_ref, edge_ref, mix_out, rate_out, wide_ref, state):
    table = mix_ref[...]
    high, mid, _ = split3(table)
    part = lane_index(table.shape) // PADDED
    mix_out[...] = jnp.where(part == 2, mid.astype(F32), high.astype(F32)).astype(BF16)
    rate_out[...] = jnp.broadcast_to(rate_ref[...], (PADDED, GY))
    for m in range(2):
        for row in range(16):
            put_row(state, (0, m, row), main_ref[row // 4, m, :, pl.ds((row % 4) * GY, GY)])
    for step in range(NSTEP):
        now = step % 2

        def body(pair, carry, now=now, step=step):
            row = step + 1 + 2 * pair
            results = [
                advance([state[now, m, row - 1 + i] for i in range(4)], mix_out, rate_out)
                for m in range(2)
            ]
            if step < NSTEP - 1:
                for m in range(2):
                    for i in range(2):
                        state[1 - now, m, row + i] = results[m][i]
            else:
                send_rows(results, row - 4, out_ref)
            return carry

        lax.fori_loop(0, (14 - 2 * step) // 2, body, 0)
        if step < NSTEP - 1:
            done = step + 1
            for m in range(2):
                for i, row in enumerate((done, done + 1, 14 - done, 15 - done)):
                    edge_ref[step, m, i] = state[1 - now, m, row]

    take = lax.broadcasted_iota(jnp.int32, (128, 256), 0)
    put = lane_index((128, 256))
    same = (put // 16 == take // 8) & (put % 8 == take % 8)
    spread = jnp.where(same, 1.0, 0.0).astype(BF16)
    group = (lane_index((128, 256)) // 8) % 2
    for j in range(2):
        for block in range(5):
            width = 128 if block < 4 else 608 - 512
            piece = split3(op_ref[j, :, pl.ds(block * 128, width)])
            grown = [jnp.dot(p, spread[0:width], preferred_element_type=F32) for p in piece]
            full = (grown[0] + grown[1]) + grown[2]
            wide_ref[j * 128 : (j + 1) * 128, block * 256 : (block + 1) * 256] = jnp.where(
                group == j, full, 0.0
            )


def edge_kernel(main_ref, prev_ref, next_ref, inner_ref, edge_ref, mix_ref, rate_ref, out_ref, state):
    for m in range(2):
        for i in range(4):
            cols = pl.ds(i * GY, GY)
            put_row(state, (0, 0, m, i), prev_ref[m, :, cols])
            put_row(state, (0, 1, m, 2 + i), next_ref[m, :, cols])
        for i in range(2):
            put_row(state, (0, 0, m, 4 + i), main_ref[0, m, :, pl.ds(i * GY, GY)])
            put_row(state, (0, 1, m, i), main_ref[3, m, :, pl.ds((2 + i) * GY, GY)])
    for step in range(NSTEP):
        now = step % 2

        def body(index, carry, now=now, step=step):
            side, pair = index // 2, index % 2
            results = [
                advance([state[now, side, m, 2 * pair + i] for i in range(4)], mix_ref, rate_ref)
                for m in range(2)
            ]
            if step < NSTEP - 1:
                for m in range(2):
                    for i in range(2):
                        state[1 - now, side, m, 2 * side + 2 * pair + i] = results[m][i]
            else:
                send_rows(results, 12 * side + 2 * pair, out_ref)
            return carry

        lax.fori_loop(0, 4, body, 0)
        if step < NSTEP - 1:
            for m in range(2):
                for i in range(2):
                    state[1 - now, 0, m, 4 + i] = edge_ref[step, m, i]
                    state[1 - now, 1, m, i] = edge_ref[step, m, 2 + i]

    for row in range(8):
        for tile in range(TILES):
            lanes = pl.ds(tile * 128, 128)
            out_ref[pl.ds(32 + row * 8, 8), 0, lanes] = inner_ref[pl.ds(row * 8, 8), 0, lanes]


def analysis_kernel(x_ref, wide, obs_ref, prec_ref, out_ref, pert, yref, rr, zz, ff, moved):
    low_half = lane_index((128, 128)) < 64
    rows = 128
    for tile in range(10):
        even = x_ref[:, 0, pl.ds(tile * 128, 128)]
        first = x_ref[:, 0, pl.ds((9 + tile) * 128, 128)]
        if tile < 9:
            second = x_ref[:, 0, pl.ds((10 + tile) * 128, 128)]
            odd = pltpu.roll(jnp.where(low_half, second, first), 64, 1)
        else:
            even = jnp.where(low_half, even, 0.0)
            odd = jnp.where(low_half, pltpu.roll(first, 64, 1), 0.0)
        mean = (jnp.sum(even, axis=0, keepdims=True) + jnp.sum(odd, axis=0, keepdims=True)) / MEMBERS
        lanes = pl.ds(tile * 128, 128)
        pert[0:rows, lanes] = even - mean
        pert[rows : 2 * rows, lanes] = odd - mean
        pert[2 * rows : 2 * rows + 8, lanes] = jnp.broadcast_to(mean, (8, 128))

    yref[...] = lax.dot_general(
        pert[...], wide[...], (((1,), (1,)), ((), ())), precision=HIGHEST, preferred_element_type=F32
    )
    eye = jnp.where(
        lax.broadcasted_iota(jnp.int32, (MEMBERS, MEMBERS), 0) == lane_index((MEMBERS, MEMBERS)), 1.0, 0.0
    )

    def mm(a, b):
        return jnp.dot(a, b, precision=HIGHEST, preferred_element_type=F32)

    scale = []
    for j in range(2):
        obs = slice(j * 128, (j + 1) * 128)
        y = yref[0:MEMBERS, obs]
        weighted = y * prec_ref[j : j + 1, :]
        gram = lax.dot_general(
            weighted, y, (((1,), (1,)), ((), ())), precision=HIGHEST, preferred_element_type=F32
        )
        system = (MEMBERS - 1.0) * eye + gram
        norm = jnp.sqrt(jnp.sum(jnp.sum(system * system, axis=0, keepdims=True), axis=1, keepdims=True))
        scale.append(norm)
        start = system / norm
        factor = 0.5 * (3.0 * eye - start)
        ff[j] = start
        zz[j] = factor
        rr[j] = mm(start, factor)

    def body(step, carry):
        for j in range(2):
            ff[j] = 0.5 * (3.0 * eye - mm(zz[j], rr[j]))
        for j in range(2):
            rr[j] = mm(rr[j], ff[j])
        for j in range(2):
            zz[j] = mm(ff[j], zz[j])
        return carry

    lax.fori_loop(0, ITERS - 2, body, 0)
    shifts = []
    for j in range(2):
        factor = 0.5 * (3.0 * eye - mm(zz[j], rr[j]))
        root = mm(factor, zz[j]) / jnp.sqrt(scale[j])
        obs = slice(j * 128, (j + 1) * 128)
        y = yref[0:MEMBERS, obs]
        innovation = obs_ref[j : j + 1, :] - yref[MEMBERS : MEMBERS + 1, obs]
        pull = jnp.sum(y * prec_ref[j : j + 1, :] * innovation, axis=1, keepdims=True)
        half = jnp.sum(root * pull, axis=0, keepdims=True)
        weight = jnp.sum(root * half, axis=1, keepdims=True)
        zz[j] = math.sqrt(MEMBERS - 1.0) * root
        shifts.append(weight)
    for block in range(5):
        lanes = pl.ds(block * 256, 256)
        own = (lane_index((MEMBERS, 256)) // 8) % 2 == 0
        cells = pert[0:MEMBERS, lanes]
        terms = []
        for j in range(2):
            base = pert[MEMBERS : MEMBERS + 1, lanes] + jnp.sum(cells * shifts[j], axis=0, keepdims=True)
            terms.append(base + mm(zz[j], cells))
        moved[:, lanes] = jnp.where(own, terms[0], terms[1])
    for tile in range(TILES):
        if tile < 9:
            value = moved[0:rows, tile * 128 : (tile + 1) * 128]
        elif tile == 9:
            rolled = pltpu.roll(moved[rows : 2 * rows, 0:128], 64, 1)
            value = jnp.where(low_half, moved[0:rows, 9 * 128 : 10 * 128], rolled)
        else:
            i = tile - 10
            first = moved[rows : 2 * rows, i * 128 : (i + 1) * 128]
            second = moved[rows : 2 * rows, (i + 1) * 128 : (i + 2) * 128]
            value = pltpu.roll(jnp.where(low_half, second, first), 64, 1)
        for s in range(4):
            out_ref[:, 0, pl.ds(s * PAIR + tile * 128, 128)] = value[s * 32 : (s + 1) * 32]


def restore_kernel(in_ref, out_ref):
    def body(s, carry):
        for y in range(4):
            tiles = [
                in_ref[pl.ds(y * 8, 8), 0, pl.ds(pl.multiple_of(s * PAIR + tile * 128, 128), 128)]
                for tile in range(TILES)
            ]
            moved = swap_blocks(jnp.stack(tiles, axis=0)).reshape(2 * LEVELS, GY)
            out_ref[2 * s, :, y * GY : (y + 1) * GY] = moved[0:LEVELS]
            out_ref[2 * s + 1, :, y * GY : (y + 1) * GY] = moved[LEVELS : 2 * LEVELS]
        return carry

    lax.fori_loop(0, 4, body, 0)


def params():
    return pltpu.CompilerParams(vmem_limit_bytes=VMEM_LIMIT)


def forecast_interior(main, mixing, rate, operator):
    return pl.pallas_call(
        interior_kernel,
        out_shape=[
            jax.ShapeDtypeStruct((64, 1, PAIR), F32),
            jax.ShapeDtypeStruct((NSTEP - 1, 2, 4, PADDED, GY), F32),
            jax.ShapeDtypeStruct((PADDED, 3 * PADDED), BF16),
            jax.ShapeDtypeStruct((PADDED, GY), F32),
            jax.ShapeDtypeStruct((2 * 128, LANES), F32),
        ],
        scratch_shapes=[pltpu.VMEM((2, 2, 16, PADDED, GY), F32)],
        compiler_params=params(),
        cost_estimate=pl.CostEstimate(flops=10**10, bytes_accessed=8 * 2**20, transcendentals=0),
        name="interior",
    )(main, mixing, rate, operator)


def forecast_edges(main, before, after, inner, edges, mixing, rate):
    return pl.pallas_call(
        edge_kernel,
        out_shape=jax.ShapeDtypeStruct((128, 1, PAIR), F32),
        scratch_shapes=[pltpu.VMEM((2, 2, 2, 6, PADDED, GY), F32)],
        compiler_params=params(),
        name="edges",
    )(main, before, after, inner, edges, mixing, rate)


def analyse(cells, operator, observed, precisions):
    return pl.pallas_call(
        analysis_kernel,
        out_shape=jax.ShapeDtypeStruct((32, 1, 4 * PAIR), F32),
        scratch_shapes=[
            pltpu.VMEM((MEMBERS + 8, LANES), F32),
            pltpu.VMEM((MEMBERS + 8, 2 * 128), F32),
            pltpu.VMEM((2, MEMBERS, MEMBERS), F32),
            pltpu.VMEM((2, MEMBERS, MEMBERS), F32),
            pltpu.VMEM((2, MEMBERS, MEMBERS), F32),
            pltpu.VMEM((MEMBERS, LANES), F32),
        ],
        compiler_params=params(),
        name="analysis",
    )(cells, operator, observed, precisions)


def restore(cells):
    return pl.pallas_call(
        restore_kernel,
        out_shape=jax.ShapeDtypeStruct((8, LEVELS, 4 * GY), F32),
        compiler_params=params(),
        name="restore",
    )(cells)


def prepare(blending_matrix, lateral_spreading):
    extra = PADDED - LEVELS
    mixing = jnp.tile(jnp.pad(blending_matrix, ((0, extra), (0, extra))), (1, 3))
    return mixing, jnp.pad(lateral_spreading, (0, extra))[:, None]


def shards(ensemble, blending_matrix, lateral_spreading, obs_op, obs_value, obs_precision):
    mixing, rate = prepare(blending_matrix, lateral_spreading)
    split = ensemble.reshape(4, 2, LEVELS, 4 * GY)
    main = lax.all_to_all(split, "x", split_axis=0, concat_axis=0, tiled=True)
    before = lax.ppermute(main[3], "zh", [(i, (i + 1) % 4) for i in range(4)])
    after = lax.ppermute(main[0], "zh", [((i + 1) % 4, i) for i in range(4)])
    inner, edges, mixed, rates, wide = forecast_interior(main, mixing, rate, obs_op)
    sent = forecast_edges(main, before, after, inner, edges, mixed, rates)
    owned = lax.all_to_all(sent, ("x", "y", "zl", "c"), split_axis=0, concat_axis=0, tiled=True)
    result = analyse(owned, wide, obs_value, obs_precision)
    returned = lax.all_to_all(result, ("y", "zl", "c"), split_axis=0, concat_axis=0, tiled=True)
    return restore(returned)


def solution(mesh):
    fine = Mesh(mesh.devices.reshape(4, 4, 2, 4, 4), ("y", "zl", "c", "zh", "x"))
    member, region = ("y", "zl", "c"), ("zh", "x")
    return jax.shard_map(
        shards,
        mesh=fine,
        in_specs=(
            P(member, None, region),
            P(),
            P(),
            P(region + member, None, None),
            P(region + member, None),
            P(region + member, None),
        ),
        out_specs=P(member, None, region),
        check_vma=False,
    )
```

```python
import math

import jax
import jax.numpy as jnp
from jax import lax
from jax.experimental import pallas as pl
from jax.experimental.pallas import tpu as pltpu
from jax.sharding import Mesh, PartitionSpec as P

F32 = jnp.float32
BF16 = jnp.bfloat16
HIGHEST = lax.Precision.HIGHEST
LEVELS = 76
PADDED = 80
GY = 128
NSTEP = 4
ITERS = 12
MEMBERS = 256
PAIR = 2 * LEVELS * 16
TILES = PAIR // 128
HALF = LEVELS * 16
LANES = 1280
VMEM_LIMIT = 32 * 1024 * 1024


def lane_index(shape):
    return lax.broadcasted_iota(jnp.int32, shape, len(shape) - 1)


def split3(x):
    high = x.astype(BF16)
    rest = x - high.astype(F32)
    mid = rest.astype(BF16)
    low = (rest - mid.astype(F32)).astype(BF16)
    return high, mid, low


def swap_blocks(x):
    sub = lax.broadcasted_iota(jnp.int32, x.shape, 1)
    block = lane_index(x.shape) // 16
    for bit in (1, 2, 4):
        up = (sub & bit) != 0
        keep = up == ((block & bit) != 0)
        lanes = 16 * bit
        lower = pltpu.roll(pltpu.roll(x, 8 - bit, 1), lanes, 2)
        if bit == 4:
            other = lower
        else:
            upper = pltpu.roll(pltpu.roll(x, bit, 1), 128 - lanes, 2)
            other = jnp.where(up, upper, lower)
        x = jnp.where(keep, x, other)
    return x


def advance(window, mix_ref, rate_ref):
    centre = window[1:3]
    high, mid, _ = split3(jnp.concatenate(centre, axis=1))
    stacked = jnp.concatenate([high, mid, high], axis=0)
    coupled = jnp.dot(mix_ref[...], stacked, preferred_element_type=F32)
    result = []
    for i in range(2):
        cells = centre[i]
        around = window[i] + window[i + 2]
        laplace = around + pltpu.roll(cells, GY - 1, 1) + pltpu.roll(cells, 1, 1) - 4.0 * cells
        pushed = jnp.tanh(coupled[:, i * GY : (i + 1) * GY])
        result.append(cells + rate_ref[...] * laplace + 0.3 * pushed)
    return result


def send_rows(results, row, out_ref):
    for i in range(2):
        both = jnp.concatenate([results[m][i][0:LEVELS] for m in range(2)], axis=0)
        moved = swap_blocks(both.reshape(TILES, 8, GY))
        for tile in range(TILES):
            out_ref[pl.ds((row + i) * 8, 8), 0, pl.ds(tile * 128, 128)] = moved[tile]


def put_row(state_ref, index, cells):
    state_ref[index + (slice(0, LEVELS), slice(None))] = cells
    state_ref[index + (slice(LEVELS, PADDED), slice(None))] = jnp.zeros((PADDED - LEVELS, GY), F32)


def deal_kernel(in_ref, out_ref):
    for x in range(4):
        out_ref[x] = in_ref[:, 2 * x : 2 * x + 2, :]


def interior_kernel(main_ref, mix_ref, rate_ref, op_ref, out_ref, edge_ref, mix_out, rate_out, wide_ref, state):
    table = mix_ref[...]
    high, mid, _ = split3(table)
    part = lane_index(table.shape) // PADDED
    mix_out[...] = jnp.where(part == 2, mid.astype(F32), high.astype(F32)).astype(BF16)
    rate_out[...] = jnp.broadcast_to(rate_ref[...], (PADDED, GY))
    for m in range(2):
        for row in range(16):
            put_row(state, (0, m, row), main_ref[row // 4, :, m, pl.ds((row % 4) * GY, GY)])
    for step in range(NSTEP):
        now = step % 2

        def body(pair, carry, now=now, step=step):
            row = step + 1 + 2 * pair
            results = [
                advance([state[now, m, row - 1 + i] for i in range(4)], mix_out, rate_out)
                for m in range(2)
            ]
            if step < NSTEP - 1:
                for m in range(2):
                    for i in range(2):
                        state[1 - now, m, row + i] = results[m][i]
            else:
                send_rows(results, row - 4, out_ref)
            return carry

        lax.fori_loop(0, (14 - 2 * step) // 2, body, 0)
        if step < NSTEP - 1:
            done = step + 1
            for m in range(2):
                for i, row in enumerate((done, done + 1, 14 - done, 15 - done)):
                    edge_ref[step, m, i] = state[1 - now, m, row]

    take = lax.broadcasted_iota(jnp.int32, (128, 256), 0)
    put = lane_index((128, 256))
    same = (put // 16 == take // 8) & (put % 8 == take % 8)
    spread = jnp.where(same, 1.0, 0.0).astype(BF16)
    group = (lane_index((128, 256)) // 8) % 2
    for j in range(2):
        for block in range(5):
            width = 128 if block < 4 else 608 - 512
            piece = split3(op_ref[j, :, pl.ds(block * 128, width)])
            grown = [jnp.dot(p, spread[0:width], preferred_element_type=F32) for p in piece]
            full = (grown[0] + grown[1]) + grown[2]
            wide_ref[j * 128 : (j + 1) * 128, block * 256 : (block + 1) * 256] = jnp.where(
                group == j, full, 0.0
            )


def edge_kernel(main_ref, prev_ref, next_ref, inner_ref, edge_ref, mix_ref, rate_ref, out_ref, state):
    for m in range(2):
        for i in range(4):
            cols = pl.ds(i * GY, GY)
            put_row(state, (0, 0, m, i), prev_ref[:, m, cols])
            put_row(state, (0, 1, m, 2 + i), next_ref[:, m, cols])
        for i in range(2):
            put_row(state, (0, 0, m, 4 + i), main_ref[0, :, m, pl.ds(i * GY, GY)])
            put_row(state, (0, 1, m, i), main_ref[3, :, m, pl.ds((2 + i) * GY, GY)])
    for step in range(NSTEP):
        now = step % 2

        def body(index, carry, now=now, step=step):
            side, pair = index // 2, index % 2
            results = [
                advance([state[now, side, m, 2 * pair + i] for i in range(4)], mix_ref, rate_ref)
                for m in range(2)
            ]
            if step < NSTEP - 1:
                for m in range(2):
                    for i in range(2):
                        state[1 - now, side, m, 2 * side + 2 * pair + i] = results[m][i]
            else:
                send_rows(results, 12 * side + 2 * pair, out_ref)
            return carry

        lax.fori_loop(0, 4, body, 0)
        if step < NSTEP - 1:
            for m in range(2):
                for i in range(2):
                    state[1 - now, 0, m, 4 + i] = edge_ref[step, m, i]
                    state[1 - now, 1, m, i] = edge_ref[step, m, 2 + i]

    for row in range(8):
        for tile in range(TILES):
            lanes = pl.ds(tile * 128, 128)
            out_ref[pl.ds(32 + row * 8, 8), 0, lanes] = inner_ref[pl.ds(row * 8, 8), 0, lanes]


def analysis_kernel(x_ref, wide, obs_ref, prec_ref, out_ref, pert, yref, rr, zz, ff, moved, roots):
    low_half = lane_index((128, 128)) < 64
    rows = 128
    for tile in range(10):
        even = x_ref[:, 0, pl.ds(tile * 128, 128)]
        first = x_ref[:, 0, pl.ds((9 + tile) * 128, 128)]
        if tile < 9:
            second = x_ref[:, 0, pl.ds((10 + tile) * 128, 128)]
            odd = pltpu.roll(jnp.where(low_half, second, first), 64, 1)
        else:
            even = jnp.where(low_half, even, 0.0)
            odd = jnp.where(low_half, pltpu.roll(first, 64, 1), 0.0)
        mean = (jnp.sum(even, axis=0, keepdims=True) + jnp.sum(odd, axis=0, keepdims=True)) / MEMBERS
        lanes = pl.ds(tile * 128, 128)
        pert[0:rows, lanes] = even - mean
        pert[rows : 2 * rows, lanes] = odd - mean
        pert[2 * rows : 2 * rows + 8, lanes] = jnp.broadcast_to(mean, (8, 128))

    yref[...] = lax.dot_general(
        pert[...], wide[...], (((1,), (1,)), ((), ())), precision=HIGHEST, preferred_element_type=F32
    )
    eye = jnp.where(
        lax.broadcasted_iota(jnp.int32, (MEMBERS, MEMBERS), 0) == lane_index((MEMBERS, MEMBERS)), 1.0, 0.0
    )

    def mm(a, b):
        return jnp.dot(a, b, precision=HIGHEST, preferred_element_type=F32)

    scale = []
    for j in range(2):
        obs = slice(j * 128, (j + 1) * 128)
        y = yref[0:MEMBERS, obs]
        weighted = y * prec_ref[j : j + 1, :]
        gram = lax.dot_general(
            weighted, y, (((1,), (1,)), ((), ())), precision=HIGHEST, preferred_element_type=F32
        )
        system = (MEMBERS - 1.0) * eye + gram
        norm = jnp.sqrt(jnp.sum(jnp.sum(system * system, axis=0, keepdims=True), axis=1, keepdims=True))
        scale.append(norm)
        start = system / norm
        factor = 0.5 * (3.0 * eye - start)
        ff[j] = start
        zz[j] = factor
        rr[j] = mm(start, factor)

    def body(step, carry):
        for j in range(2):
            ff[j] = 0.5 * (3.0 * eye - mm(zz[j], rr[j]))
        for j in range(2):
            rr[j] = mm(rr[j], ff[j])
        for j in range(2):
            zz[j] = mm(ff[j], zz[j])
        return carry

    lax.fori_loop(0, ITERS - 2, body, 0)
    shifts = []
    for j in range(2):
        factor = 0.5 * (3.0 * eye - mm(zz[j], rr[j]))
        root = mm(factor, zz[j]) / jnp.sqrt(scale[j])
        obs = slice(j * 128, (j + 1) * 128)
        y = yref[0:MEMBERS, obs]
        innovation = obs_ref[j : j + 1, :] - yref[MEMBERS : MEMBERS + 1, obs]
        pull = jnp.sum(y * prec_ref[j : j + 1, :] * innovation, axis=1, keepdims=True)
        half = jnp.sum(root * pull, axis=0, keepdims=True)
        weight = jnp.sum(root * half, axis=1, keepdims=True)
        shifts.append(weight)
        for i, part in enumerate(split3(math.sqrt(MEMBERS - 1.0) * root)[0:2]):
            roots[i, j] = part
    for block in range(5):
        lanes = pl.ds(block * 256, 256)
        own = (lane_index((MEMBERS, 256)) // 8) % 2 == 0
        cells = pert[0:MEMBERS, lanes]
        high, mid, _ = split3(cells)
        terms = []
        for j in range(2):
            base = pert[MEMBERS : MEMBERS + 1, lanes] + jnp.sum(cells * shifts[j], axis=0, keepdims=True)
            small = jnp.dot(roots[0, j], mid, preferred_element_type=F32) + jnp.dot(
                roots[1, j], high, preferred_element_type=F32
            )
            terms.append(base + (jnp.dot(roots[0, j], high, preferred_element_type=F32) + small))
        moved[:, lanes] = jnp.where(own, terms[0], terms[1])
    lane_block = lane_index((32, 128)) // 16
    for tile in range(10):
        cols = pl.ds(tile * 128, 128)
        group = [moved[(m % 2) * rows + (m // 2) * 32 : (m % 2) * rows + (m // 2) * 32 + 32, cols] for m in range(8)]
        for bit in (1, 2, 4):
            up = (lane_block & bit) != 0
            for m in range(8):
                if m & bit:
                    continue
                low, high = group[m], group[m | bit]
                group[m] = jnp.where(up, pltpu.roll(high, 16 * bit, 1), low)
                group[m | bit] = jnp.where(up, high, pltpu.roll(low, 128 - 16 * bit, 1))
        for i in range(8 if tile < 9 else 4):
            out_ref[:, 0, pl.ds((tile * 8 + i) * 128, 128)] = group[i]


def restore_kernel(in_ref, out_ref):
    def body(y, carry):
        cols = pl.ds(pl.multiple_of(y * GY, GY), GY)
        for first in range(0, LEVELS, 19):
            tiles = [in_ref[pl.ds(y * 8, 8), 0, pl.ds((first + i) * 128, 128)] for i in range(19)]
            out_ref[first : first + 19, :, cols] = swap_blocks(jnp.stack(tiles, axis=0))
        return carry

    lax.fori_loop(0, 4, body, 0)


def params():
    return pltpu.CompilerParams(vmem_limit_bytes=VMEM_LIMIT)


def deal(cells):
    return pl.pallas_call(
        deal_kernel,
        out_shape=jax.ShapeDtypeStruct((4, LEVELS, 2, 4 * GY), F32),
        compiler_params=params(),
        name="deal",
    )(cells)


def forecast_interior(main, mixing, rate, operator):
    return pl.pallas_call(
        interior_kernel,
        out_shape=[
            jax.ShapeDtypeStruct((64, 1, PAIR), F32),
            jax.ShapeDtypeStruct((NSTEP - 1, 2, 4, PADDED, GY), F32),
            jax.ShapeDtypeStruct((PADDED, 3 * PADDED), BF16),
            jax.ShapeDtypeStruct((PADDED, GY), F32),
            jax.ShapeDtypeStruct((2 * 128, LANES), F32),
        ],
        scratch_shapes=[pltpu.VMEM((2, 2, 16, PADDED, GY), F32)],
        compiler_params=params(),
        cost_estimate=pl.CostEstimate(flops=10**10, bytes_accessed=8 * 2**20, transcendentals=0),
        name="interior",
    )(main, mixing, rate, operator)


def forecast_edges(main, before, after, inner, edges, mixing, rate):
    return pl.pallas_call(
        edge_kernel,
        out_shape=jax.ShapeDtypeStruct((128, 1, PAIR), F32),
        scratch_shapes=[pltpu.VMEM((2, 2, 2, 6, PADDED, GY), F32)],
        compiler_params=params(),
        name="edges",
    )(main, before, after, inner, edges, mixing, rate)


def analyse(cells, operator, observed, precisions):
    return pl.pallas_call(
        analysis_kernel,
        out_shape=jax.ShapeDtypeStruct((32, 1, 4 * PAIR), F32),
        scratch_shapes=[
            pltpu.VMEM((MEMBERS + 8, LANES), F32),
            pltpu.VMEM((MEMBERS + 8, 2 * 128), F32),
            pltpu.VMEM((2, MEMBERS, MEMBERS), F32),
            pltpu.VMEM((2, MEMBERS, MEMBERS), F32),
            pltpu.VMEM((2, MEMBERS, MEMBERS), F32),
            pltpu.VMEM((MEMBERS, LANES), F32),
            pltpu.VMEM((2, 2, MEMBERS, MEMBERS), BF16),
        ],
        compiler_params=params(),
        name="analysis",
    )(cells, operator, observed, precisions)


def restore(cells):
    return pl.pallas_call(
        restore_kernel,
        out_shape=jax.ShapeDtypeStruct((LEVELS, 8, 4 * GY), F32),
        compiler_params=params(),
        name="restore",
    )(cells)


def prepare(blending_matrix, lateral_spreading):
    extra = PADDED - LEVELS
    mixing = jnp.tile(jnp.pad(blending_matrix, ((0, extra), (0, extra))), (1, 3))
    return mixing, jnp.pad(lateral_spreading, (0, extra))[:, None]


def shards(ensemble, blending_matrix, lateral_spreading, obs_op, obs_value, obs_precision):
    mixing, rate = prepare(blending_matrix, lateral_spreading)
    split = deal(ensemble.transpose(1, 0, 2))
    main = lax.all_to_all(split, "x", split_axis=0, concat_axis=0, tiled=True)
    before = lax.ppermute(main[3], "zh", [(i, (i + 1) % 4) for i in range(4)])
    after = lax.ppermute(main[0], "zh", [((i + 1) % 4, i) for i in range(4)])
    inner, edges, mixed, rates, wide = forecast_interior(main, mixing, rate, obs_op)
    sent = forecast_edges(main, before, after, inner, edges, mixed, rates)
    owned = lax.all_to_all(sent, ("x", "y", "zl", "c"), split_axis=0, concat_axis=0, tiled=True)
    result = analyse(owned, wide, obs_value, obs_precision)
    returned = lax.all_to_all(result, ("y", "zl", "c"), split_axis=0, concat_axis=0, tiled=True)
    return restore(returned).transpose(1, 0, 2)


def solution(mesh):
    fine = Mesh(mesh.devices.reshape(4, 4, 2, 4, 4), ("y", "zl", "c", "zh", "x"))
    member, region = ("y", "zl", "c"), ("zh", "x")
    return jax.shard_map(
        shards,
        mesh=fine,
        in_specs=(
            P(member, None, region),
            P(),
            P(),
            P(region + member, None, None),
            P(region + member, None),
            P(region + member, None),
        ),
        out_specs=P(member, None, region),
        check_vma=False,
    )
```

```python
import math

import jax
import jax.numpy as jnp
from jax import lax
from jax.experimental import pallas as pl
from jax.experimental.pallas import tpu as pltpu
from jax.sharding import Mesh, PartitionSpec as P

F32 = jnp.float32
BF16 = jnp.bfloat16
HIGHEST = lax.Precision.HIGHEST
LEVELS = 76
PADDED = 80
GY = 128
NSTEP = 4
ITERS = 12
MEMBERS = 256
PAIR = 2 * LEVELS * 16
TILES = PAIR // 128
HALF = LEVELS * 16
LANES = 1280
VMEM_LIMIT = 32 * 1024 * 1024


def lane_index(shape):
    return lax.broadcasted_iota(jnp.int32, shape, len(shape) - 1)


def split3(x):
    high = x.astype(BF16)
    rest = x - high.astype(F32)
    mid = rest.astype(BF16)
    low = (rest - mid.astype(F32)).astype(BF16)
    return high, mid, low


def swap_blocks(x):
    sub = lax.broadcasted_iota(jnp.int32, x.shape, 1)
    block = lane_index(x.shape) // 16
    for bit in (1, 2, 4):
        up = (sub & bit) != 0
        keep = up == ((block & bit) != 0)
        lanes = 16 * bit
        lower = pltpu.roll(pltpu.roll(x, 8 - bit, 1), lanes, 2)
        if bit == 4:
            other = lower
        else:
            upper = pltpu.roll(pltpu.roll(x, bit, 1), 128 - lanes, 2)
            other = jnp.where(up, upper, lower)
        x = jnp.where(keep, x, other)
    return x


def advance(window, mix_ref, rate_ref):
    centre = window[1:3]
    high, mid, _ = split3(jnp.concatenate(centre, axis=1))
    stacked = jnp.concatenate([high, mid, high], axis=0)
    coupled = jnp.dot(mix_ref[...], stacked, preferred_element_type=F32)
    result = []
    for i in range(2):
        cells = centre[i]
        around = window[i] + window[i + 2]
        laplace = around + pltpu.roll(cells, GY - 1, 1) + pltpu.roll(cells, 1, 1) - 4.0 * cells
        pushed = jnp.tanh(coupled[:, i * GY : (i + 1) * GY])
        result.append(cells + rate_ref[...] * laplace + 0.3 * pushed)
    return result


def send_rows(results, row, out_ref):
    for i in range(2):
        both = jnp.concatenate([results[m][i][0:LEVELS] for m in range(2)], axis=0)
        moved = swap_blocks(both.reshape(TILES, 8, GY))
        for tile in range(TILES):
            out_ref[pl.ds((row + i) * 8, 8), 0, pl.ds(tile * 128, 128)] = moved[tile]


def put_row(state_ref, index, cells):
    state_ref[index + (slice(0, LEVELS), slice(None))] = cells
    state_ref[index + (slice(LEVELS, PADDED), slice(None))] = jnp.zeros((PADDED - LEVELS, GY), F32)


def deal_kernel(in_ref, out_ref):
    for x in range(4):
        out_ref[x] = in_ref[:, 2 * x : 2 * x + 2, :]


def interior_kernel(main_ref, mix_ref, rate_ref, op_ref, out_ref, edge_ref, mix_out, rate_out, wide_ref, state):
    table = mix_ref[...]
    high, mid, _ = split3(table)
    part = lane_index(table.shape) // PADDED
    mix_out[...] = jnp.where(part == 2, mid.astype(F32), high.astype(F32)).astype(BF16)
    rate_out[...] = jnp.broadcast_to(rate_ref[...], (PADDED, GY))
    for m in range(2):
        for row in range(16):
            put_row(state, (0, m, row), main_ref[row // 4, :, m, pl.ds((row % 4) * GY, GY)])
    for step in range(NSTEP):
        now = step % 2

        def body(pair, carry, now=now, step=step):
            row = step + 1 + 2 * pair
            results = [
                advance([state[now, m, row - 1 + i] for i in range(4)], mix_out, rate_out)
                for m in range(2)
            ]
            if step < NSTEP - 1:
                for m in range(2):
                    for i in range(2):
                        state[1 - now, m, row + i] = results[m][i]
            else:
                send_rows(results, row - 4, out_ref)
            return carry

        lax.fori_loop(0, (14 - 2 * step) // 2, body, 0)
        if step < NSTEP - 1:
            done = step + 1
            for m in range(2):
                for i, row in enumerate((done, done + 1, 14 - done, 15 - done)):
                    edge_ref[step, m, i] = state[1 - now, m, row]

    take = lax.broadcasted_iota(jnp.int32, (128, 256), 0)
    put = lane_index((128, 256))
    same = (put // 16 == take // 8) & (put % 8 == take % 8)
    spread = jnp.where(same, 1.0, 0.0).astype(BF16)
    group = (lane_index((128, 256)) // 8) % 2
    for j in range(2):
        for block in range(5):
            width = 128 if block < 4 else 608 - 512
            piece = split3(op_ref[j, :, pl.ds(block * 128, width)])
            grown = [jnp.dot(p, spread[0:width], preferred_element_type=F32) for p in piece]
            full = (grown[0] + grown[1]) + grown[2]
            wide_ref[j * 128 : (j + 1) * 128, block * 256 : (block + 1) * 256] = jnp.where(
                group == j, full, 0.0
            )


def edge_kernel(main_ref, next_ref, prev_ref, inner_ref, edge_ref, mix_ref, rate_ref, out_ref, state, sem):
    inner = pltpu.make_async_copy(inner_ref, out_ref.at[pl.ds(32, 64)], sem)
    inner.start()
    for m in range(2):
        for i in range(4):
            cols = pl.ds(i * GY, GY)
            put_row(state, (0, 0, m, i), prev_ref[:, m, cols])
            put_row(state, (0, 1, m, 2 + i), next_ref[:, m, cols])
        for i in range(2):
            put_row(state, (0, 0, m, 4 + i), main_ref[0, :, m, pl.ds(i * GY, GY)])
            put_row(state, (0, 1, m, i), main_ref[3, :, m, pl.ds((2 + i) * GY, GY)])
    for step in range(NSTEP):
        now = step % 2

        def body(index, carry, now=now, step=step):
            side, pair = index // 2, index % 2
            results = [
                advance([state[now, side, m, 2 * pair + i] for i in range(4)], mix_ref, rate_ref)
                for m in range(2)
            ]
            if step < NSTEP - 1:
                for m in range(2):
                    for i in range(2):
                        state[1 - now, side, m, 2 * side + 2 * pair + i] = results[m][i]
            else:
                send_rows(results, 12 * side + 2 * pair, out_ref)
            return carry

        lax.fori_loop(0, 4, body, 0)
        if step < NSTEP - 1:
            for m in range(2):
                for i in range(2):
                    state[1 - now, 0, m, 4 + i] = edge_ref[step, m, i]
                    state[1 - now, 1, m, i] = edge_ref[step, m, 2 + i]

    inner.wait()


def analysis_kernel(x_ref, wide, obs_ref, prec_ref, out_ref, pert, yref, moved, roots, *parts):
    low_half = lane_index((128, 128)) < 64
    rows = 128
    for tile in range(10):
        even = x_ref[:, 0, pl.ds(tile * 128, 128)]
        first = x_ref[:, 0, pl.ds((9 + tile) * 128, 128)]
        if tile < 9:
            second = x_ref[:, 0, pl.ds((10 + tile) * 128, 128)]
            odd = pltpu.roll(jnp.where(low_half, second, first), 64, 1)
        else:
            even = jnp.where(low_half, even, 0.0)
            odd = jnp.where(low_half, pltpu.roll(first, 64, 1), 0.0)
        mean = (jnp.sum(even, axis=0, keepdims=True) + jnp.sum(odd, axis=0, keepdims=True)) / MEMBERS
        lanes = pl.ds(tile * 128, 128)
        pert[0:rows, lanes] = even - mean
        pert[rows : 2 * rows, lanes] = odd - mean
        pert[2 * rows : 2 * rows + 8, lanes] = jnp.broadcast_to(mean, (8, 128))

    yref[...] = lax.dot_general(
        pert[...], wide[...], (((1,), (1,)), ((), ())), precision=HIGHEST, preferred_element_type=F32
    )
    eye = jnp.where(
        lax.broadcasted_iota(jnp.int32, (MEMBERS, MEMBERS), 0) == lane_index((MEMBERS, MEMBERS)), 1.0, 0.0
    )

    def mm(a, b):
        return jnp.dot(a, b, precision=HIGHEST, preferred_element_type=F32)

    def put(refs, x):
        for ref, part in zip(refs, split3(x)):
            ref[...] = part

    def product(a, b):
        total = None
        for i, k in ((2, 0), (0, 2), (1, 1), (1, 0), (0, 1), (0, 0)):
            term = jnp.dot(a[i][...], b[k][...], preferred_element_type=F32)
            total = term if total is None else term + total
        return total

    rr, zz, ff = [[parts[9 * j + 3 * i : 9 * j + 3 * i + 3] for j in range(2)] for i in range(3)]
    scale = []
    for j in range(2):
        obs = slice(j * 128, (j + 1) * 128)
        y = yref[0:MEMBERS, obs]
        weighted = y * prec_ref[j : j + 1, :]
        gram = lax.dot_general(
            weighted, y, (((1,), (1,)), ((), ())), precision=HIGHEST, preferred_element_type=F32
        )
        system = (MEMBERS - 1.0) * eye + gram
        norm = jnp.sqrt(jnp.sum(jnp.sum(system * system, axis=0, keepdims=True), axis=1, keepdims=True))
        scale.append(norm)
        start = system / norm
        factor = 0.5 * (3.0 * eye - start)
        put(zz[j], factor)
        put(rr[j], mm(start, factor))

    def newton(last=False):
        for j in range(2):
            put(ff[j], 0.5 * (3.0 * eye - product(zz[j], rr[j])))
        if last:
            return [product(ff[j], zz[j]) for j in range(2)]
        for j in range(2):
            put(rr[j], product(rr[j], ff[j]))
        for j in range(2):
            put(zz[j], product(ff[j], zz[j]))
        return None

    def body(step, carry):
        newton()
        return carry

    lax.fori_loop(0, ITERS - 2, body, 0)
    ends = newton(last=True)
    shifts = []
    for j in range(2):
        root = ends[j] / jnp.sqrt(scale[j])
        obs = slice(j * 128, (j + 1) * 128)
        y = yref[0:MEMBERS, obs]
        innovation = obs_ref[j : j + 1, :] - yref[MEMBERS : MEMBERS + 1, obs]
        pull = jnp.sum(y * prec_ref[j : j + 1, :] * innovation, axis=1, keepdims=True)
        half = jnp.sum(root * pull, axis=0, keepdims=True)
        weight = jnp.sum(root * half, axis=1, keepdims=True)
        shifts.append(weight)
        for i, part in enumerate(split3(math.sqrt(MEMBERS - 1.0) * root)[0:2]):
            roots[i, j] = part
    for block in range(5):
        lanes = pl.ds(block * 256, 256)
        own = (lane_index((MEMBERS, 256)) // 8) % 2 == 0
        cells = pert[0:MEMBERS, lanes]
        high, mid, _ = split3(cells)
        terms = []
        for j in range(2):
            base = pert[MEMBERS : MEMBERS + 1, lanes] + jnp.sum(cells * shifts[j], axis=0, keepdims=True)
            small = jnp.dot(roots[0, j], mid, preferred_element_type=F32) + jnp.dot(
                roots[1, j], high, preferred_element_type=F32
            )
            terms.append(base + (jnp.dot(roots[0, j], high, preferred_element_type=F32) + small))
        moved[:, lanes] = jnp.where(own, terms[0], terms[1])
    lane_block = lane_index((32, 128)) // 16
    for tile in range(10):
        cols = pl.ds(tile * 128, 128)
        group = [moved[(m % 2) * rows + (m // 2) * 32 : (m % 2) * rows + (m // 2) * 32 + 32, cols] for m in range(8)]
        for bit in (1, 2, 4):
            up = (lane_block & bit) != 0
            for m in range(8):
                if m & bit:
                    continue
                low, high = group[m], group[m | bit]
                group[m] = jnp.where(up, pltpu.roll(high, 16 * bit, 1), low)
                group[m | bit] = jnp.where(up, high, pltpu.roll(low, 128 - 16 * bit, 1))
        for i in range(8 if tile < 9 else 4):
            out_ref[:, 0, pl.ds((tile * 8 + i) * 128, 128)] = group[i]


def restore_kernel(in_ref, out_ref):
    for first in range(0, LEVELS, 19):
        tiles = [in_ref[:, 0, pl.ds((first + i) * 128, 128)] for i in range(19)]
        out_ref[first : first + 19] = swap_blocks(jnp.stack(tiles, axis=0))


def params():
    return pltpu.CompilerParams(vmem_limit_bytes=VMEM_LIMIT)


def deal(cells):
    return pl.pallas_call(
        deal_kernel,
        out_shape=jax.ShapeDtypeStruct((4, LEVELS, 2, 4 * GY), F32),
        compiler_params=params(),
        name="deal",
    )(cells)


def forecast_interior(main, mixing, rate, operator):
    return pl.pallas_call(
        interior_kernel,
        out_shape=[
            jax.ShapeDtypeStruct((64, 1, PAIR), F32),
            jax.ShapeDtypeStruct((NSTEP - 1, 2, 4, PADDED, GY), F32),
            jax.ShapeDtypeStruct((PADDED, 3 * PADDED), BF16),
            jax.ShapeDtypeStruct((PADDED, GY), F32),
            jax.ShapeDtypeStruct((2 * 128, LANES), F32),
        ],
        scratch_shapes=[pltpu.VMEM((2, 2, 16, PADDED, GY), F32)],
        compiler_params=params(),
        cost_estimate=pl.CostEstimate(flops=10**10, bytes_accessed=8 * 2**20, transcendentals=0),
        name="interior",
    )(main, mixing, rate, operator)


def forecast_edges(main, before, after, inner, edges, mixing, rate):
    return pl.pallas_call(
        edge_kernel,
        out_shape=jax.ShapeDtypeStruct((128, 1, PAIR), F32),
        scratch_shapes=[pltpu.VMEM((2, 2, 2, 6, PADDED, GY), F32), pltpu.SemaphoreType.DMA],
        compiler_params=params(),
        name="edges",
    )(main, after, before, inner, edges, mixing, rate)


def analyse(cells, operator, observed, precisions):
    return pl.pallas_call(
        analysis_kernel,
        out_shape=jax.ShapeDtypeStruct((32, 1, 4 * PAIR), F32),
        scratch_shapes=[
            pltpu.VMEM((MEMBERS + 8, LANES), F32),
            pltpu.VMEM((MEMBERS + 8, 2 * 128), F32),
            pltpu.VMEM((MEMBERS, LANES), F32),
            pltpu.VMEM((2, 2, MEMBERS, MEMBERS), BF16),
            *([pltpu.VMEM((MEMBERS, MEMBERS), BF16)] * 18),
        ],
        compiler_params=params(),
        name="analysis",
    )(cells, operator, observed, precisions)


def restore(cells):
    return pl.pallas_call(
        restore_kernel,
        grid=(4,),
        in_specs=[pl.BlockSpec((8, 1, 4 * PAIR), lambda y: (y, 0, 0))],
        out_specs=pl.BlockSpec((LEVELS, 8, GY), lambda y: (0, 0, y)),
        out_shape=jax.ShapeDtypeStruct((LEVELS, 8, 4 * GY), F32),
        compiler_params=params(),
        name="restore",
    )(cells)


def prepare(blending_matrix, lateral_spreading):
    extra = PADDED - LEVELS
    mixing = jnp.tile(jnp.pad(blending_matrix, ((0, extra), (0, extra))), (1, 3))
    return mixing, jnp.pad(lateral_spreading, (0, extra))[:, None]


def shards(ensemble, blending_matrix, lateral_spreading, obs_op, obs_value, obs_precision):
    mixing, rate = prepare(blending_matrix, lateral_spreading)
    split = deal(ensemble.transpose(1, 0, 2))
    main = lax.all_to_all(split, "x", split_axis=0, concat_axis=0, tiled=True)
    after = lax.ppermute(main[0], "zh", [((i + 1) % 4, i) for i in range(4)])
    before = lax.ppermute(main[3], "zh", [(i, (i + 1) % 4) for i in range(4)])
    inner, edges, mixed, rates, wide = forecast_interior(main, mixing, rate, obs_op)
    sent = forecast_edges(main, before, after, inner, edges, mixed, rates)
    owned = lax.all_to_all(sent, ("x", "y", "zl", "c"), split_axis=0, concat_axis=0, tiled=True)
    result = analyse(owned, wide, obs_value, obs_precision)
    returned = lax.all_to_all(result, ("y", "zl", "c"), split_axis=0, concat_axis=0, tiled=True)
    return restore(returned).transpose(1, 0, 2)


def solution(mesh):
    fine = Mesh(mesh.devices.reshape(4, 4, 2, 4, 4), ("y", "zl", "c", "zh", "x"))
    member, region = ("y", "zl", "c"), ("zh", "x")
    return jax.shard_map(
        shards,
        mesh=fine,
        in_specs=(
            P(member, None, region),
            P(),
            P(),
            P(region + member, None, None),
            P(region + member, None),
            P(region + member, None),
        ),
        out_specs=P(member, None, region),
        check_vma=False,
    )
```

```python
import math

import jax
import jax.numpy as jnp
from jax import lax
from jax.experimental import pallas as pl
from jax.experimental.pallas import tpu as pltpu
from jax.sharding import Mesh, PartitionSpec as P

F32 = jnp.float32
BF16 = jnp.bfloat16
HIGHEST = lax.Precision.HIGHEST
LEVELS = 76
PADDED = 80
GY = 128
NSTEP = 4
ITERS = 12
MEMBERS = 256
PAIR = 2 * LEVELS * 16
TILES = PAIR // 128
HALF = LEVELS * 16
LANES = 1280
VMEM_LIMIT = 32 * 1024 * 1024


def lane_index(shape):
    return lax.broadcasted_iota(jnp.int32, shape, len(shape) - 1)


def split3(x):
    high = x.astype(BF16)
    rest = x - high.astype(F32)
    mid = rest.astype(BF16)
    low = (rest - mid.astype(F32)).astype(BF16)
    return high, mid, low


def swap_blocks(tiles):
    sub = lax.broadcasted_iota(jnp.int32, (8, 128), 0)
    lane = lane_index((8, 128))
    block, col = lane // 16, lane % 16
    skew = ((block + sub) % 8) * 16 + col
    turn = (sub - block) % 8
    back = turn * 16 + col
    result = []
    for x in tiles:
        for index, axis in ((skew, 1), (turn, 0), (back, 1)):
            x = jnp.take_along_axis(x, index, axis=axis, mode="promise_in_bounds")
        result.append(x)
    return result


def advance(window, mix_ref, rate_ref):
    centre = window[1:3]
    high, mid, _ = split3(jnp.concatenate(centre, axis=1))
    stacked = jnp.concatenate([high, mid, high], axis=0)
    coupled = jnp.dot(mix_ref[...], stacked, preferred_element_type=F32)
    result = []
    for i in range(2):
        cells = centre[i]
        around = window[i] + window[i + 2]
        laplace = around + pltpu.roll(cells, GY - 1, 1) + pltpu.roll(cells, 1, 1) - 4.0 * cells
        pushed = jnp.tanh(coupled[:, i * GY : (i + 1) * GY])
        result.append(cells + rate_ref[...] * laplace + 0.3 * pushed)
    return result


def send_rows(results, row, out_ref):
    for i in range(2):
        both = jnp.concatenate([results[m][i][0:LEVELS] for m in range(2)], axis=0)
        moved = swap_blocks([both[tile * 8 : tile * 8 + 8] for tile in range(TILES)])
        for tile in range(TILES):
            out_ref[pl.ds((row + i) * 8, 8), 0, pl.ds(tile * 128, 128)] = moved[tile]


def put_row(state_ref, index, cells):
    state_ref[index + (slice(0, LEVELS), slice(None))] = cells
    state_ref[index + (slice(LEVELS, PADDED), slice(None))] = jnp.zeros((PADDED - LEVELS, GY), F32)


def deal_kernel(in_ref, out_ref):
    for x in range(4):
        out_ref[x] = in_ref[:, 2 * x : 2 * x + 2, :]


def interior_kernel(main_ref, mix_ref, rate_ref, op_ref, out_ref, edge_ref, mix_out, rate_out, wide_ref, state):
    table = mix_ref[...]
    high, mid, _ = split3(table)
    part = lane_index(table.shape) // PADDED
    mix_out[...] = jnp.where(part == 2, mid.astype(F32), high.astype(F32)).astype(BF16)
    rate_out[...] = jnp.broadcast_to(rate_ref[...], (PADDED, GY))
    for m in range(2):
        for row in range(16):
            put_row(state, (0, m, row), main_ref[row // 4, :, m, pl.ds((row % 4) * GY, GY)])
    for step in range(NSTEP):
        now = step % 2

        def body(pair, carry, now=now, step=step):
            row = step + 1 + 2 * pair
            results = [
                advance([state[now, m, row - 1 + i] for i in range(4)], mix_out, rate_out)
                for m in range(2)
            ]
            if step < NSTEP - 1:
                for m in range(2):
                    for i in range(2):
                        state[1 - now, m, row + i] = results[m][i]
            else:
                send_rows(results, row - 4, out_ref)
            return carry

        lax.fori_loop(0, (14 - 2 * step) // 2, body, 0)
        if step < NSTEP - 1:
            done = step + 1
            for m in range(2):
                for i, row in enumerate((done, done + 1, 14 - done, 15 - done)):
                    edge_ref[step, m, i] = state[1 - now, m, row]

    take = lax.broadcasted_iota(jnp.int32, (128, 256), 0)
    put = lane_index((128, 256))
    same = (put // 16 == take // 8) & (put % 8 == take % 8)
    spread = jnp.where(same, 1.0, 0.0).astype(BF16)
    group = (lane_index((128, 256)) // 8) % 2
    for j in range(2):
        for block in range(5):
            width = 128 if block < 4 else 608 - 512
            piece = split3(op_ref[j, :, pl.ds(block * 128, width)])
            grown = [jnp.dot(p, spread[0:width], preferred_element_type=F32) for p in piece]
            full = (grown[0] + grown[1]) + grown[2]
            wide_ref[j * 128 : (j + 1) * 128, block * 256 : (block + 1) * 256] = jnp.where(
                group == j, full, 0.0
            )


def edge_kernel(main_ref, next_ref, prev_ref, inner_ref, edge_ref, mix_ref, rate_ref, out_ref, state, sem):
    inner = pltpu.make_async_copy(inner_ref, out_ref.at[pl.ds(32, 64)], sem)
    inner.start()
    for m in range(2):
        for i in range(4):
            cols = pl.ds(i * GY, GY)
            put_row(state, (0, 0, m, i), prev_ref[:, m, cols])
            put_row(state, (0, 1, m, 2 + i), next_ref[:, m, cols])
        for i in range(2):
            put_row(state, (0, 0, m, 4 + i), main_ref[0, :, m, pl.ds(i * GY, GY)])
            put_row(state, (0, 1, m, i), main_ref[3, :, m, pl.ds((2 + i) * GY, GY)])
    for step in range(NSTEP):
        now = step % 2

        def body(index, carry, now=now, step=step):
            side, pair = index // 2, index % 2
            results = [
                advance([state[now, side, m, 2 * pair + i] for i in range(4)], mix_ref, rate_ref)
                for m in range(2)
            ]
            if step < NSTEP - 1:
                for m in range(2):
                    for i in range(2):
                        state[1 - now, side, m, 2 * side + 2 * pair + i] = results[m][i]
            else:
                send_rows(results, 12 * side + 2 * pair, out_ref)
            return carry

        lax.fori_loop(0, 4, body, 0)
        if step < NSTEP - 1:
            for m in range(2):
                for i in range(2):
                    state[1 - now, 0, m, 4 + i] = edge_ref[step, m, i]
                    state[1 - now, 1, m, i] = edge_ref[step, m, 2 + i]

    inner.wait()


def analysis_kernel(x_ref, wide, obs_ref, prec_ref, out_ref, pert, yref, moved, roots, *parts):
    low_half = lane_index((128, 128)) < 64
    rows = 128
    for tile in range(10):
        even = x_ref[:, 0, pl.ds(tile * 128, 128)]
        first = x_ref[:, 0, pl.ds((9 + tile) * 128, 128)]
        if tile < 9:
            second = x_ref[:, 0, pl.ds((10 + tile) * 128, 128)]
            odd = pltpu.roll(jnp.where(low_half, second, first), 64, 1)
        else:
            even = jnp.where(low_half, even, 0.0)
            odd = jnp.where(low_half, pltpu.roll(first, 64, 1), 0.0)
        mean = (jnp.sum(even, axis=0, keepdims=True) + jnp.sum(odd, axis=0, keepdims=True)) / MEMBERS
        lanes = pl.ds(tile * 128, 128)
        pert[0:rows, lanes] = even - mean
        pert[rows : 2 * rows, lanes] = odd - mean
        pert[2 * rows : 2 * rows + 8, lanes] = jnp.broadcast_to(mean, (8, 128))

    yref[...] = lax.dot_general(
        pert[...], wide[...], (((1,), (1,)), ((), ())), precision=HIGHEST, preferred_element_type=F32
    )
    eye = jnp.where(
        lax.broadcasted_iota(jnp.int32, (MEMBERS, MEMBERS), 0) == lane_index((MEMBERS, MEMBERS)), 1.0, 0.0
    )

    def mm(a, b):
        return jnp.dot(a, b, precision=HIGHEST, preferred_element_type=F32)

    def put(refs, x):
        for ref, part in zip(refs, split3(x)):
            ref[...] = part

    def product(a, b):
        total = None
        for i, k in ((2, 0), (0, 2), (1, 1), (1, 0), (0, 1), (0, 0)):
            term = jnp.dot(a[i][...], b[k][...], preferred_element_type=F32)
            total = term if total is None else term + total
        return total

    rr, zz, ff = [[parts[9 * j + 3 * i : 9 * j + 3 * i + 3] for j in range(2)] for i in range(3)]
    scale = []
    for j in range(2):
        obs = slice(j * 128, (j + 1) * 128)
        y = yref[0:MEMBERS, obs]
        weighted = y * prec_ref[j : j + 1, :]
        gram = lax.dot_general(
            weighted, y, (((1,), (1,)), ((), ())), precision=HIGHEST, preferred_element_type=F32
        )
        system = (MEMBERS - 1.0) * eye + gram
        norm = jnp.sqrt(jnp.sum(jnp.sum(system * system, axis=0, keepdims=True), axis=1, keepdims=True))
        scale.append(norm)
        start = system / norm
        factor = 0.5 * (3.0 * eye - start)
        put(zz[j], factor)
        put(rr[j], mm(start, factor))

    def newton(last=False):
        for j in range(2):
            put(ff[j], 0.5 * (3.0 * eye - product(zz[j], rr[j])))
        if last:
            return [product(ff[j], zz[j]) for j in range(2)]
        for j in range(2):
            put(rr[j], product(rr[j], ff[j]))
        for j in range(2):
            put(zz[j], product(ff[j], zz[j]))
        return None

    def body(step, carry):
        newton()
        return carry

    lax.fori_loop(0, ITERS - 2, body, 0)
    ends = newton(last=True)
    shifts = []
    for j in range(2):
        root = ends[j] / jnp.sqrt(scale[j])
        obs = slice(j * 128, (j + 1) * 128)
        y = yref[0:MEMBERS, obs]
        innovation = obs_ref[j : j + 1, :] - yref[MEMBERS : MEMBERS + 1, obs]
        pull = jnp.sum(y * prec_ref[j : j + 1, :] * innovation, axis=1, keepdims=True)
        half = jnp.sum(root * pull, axis=0, keepdims=True)
        weight = jnp.sum(root * half, axis=1, keepdims=True)
        shifts.append(weight)
        for i, part in enumerate(split3(math.sqrt(MEMBERS - 1.0) * root)[0:2]):
            roots[i, j] = part
    for block in range(5):
        lanes = pl.ds(block * 256, 256)
        own = (lane_index((MEMBERS, 256)) // 8) % 2 == 0
        cells = pert[0:MEMBERS, lanes]
        high, mid, _ = split3(cells)
        terms = []
        for j in range(2):
            base = pert[MEMBERS : MEMBERS + 1, lanes] + jnp.sum(cells * shifts[j], axis=0, keepdims=True)
            small = jnp.dot(roots[0, j], mid, preferred_element_type=F32) + jnp.dot(
                roots[1, j], high, preferred_element_type=F32
            )
            terms.append(base + (jnp.dot(roots[0, j], high, preferred_element_type=F32) + small))
        moved[:, lanes] = jnp.where(own, terms[0], terms[1])
    lane_block = lane_index((32, 128)) // 16
    for tile in range(10):
        cols = pl.ds(tile * 128, 128)
        group = [moved[(m % 2) * rows + (m // 2) * 32 : (m % 2) * rows + (m // 2) * 32 + 32, cols] for m in range(8)]
        for bit in (1, 2, 4):
            up = (lane_block & bit) != 0
            for m in range(8):
                if m & bit:
                    continue
                low, high = group[m], group[m | bit]
                group[m] = jnp.where(up, pltpu.roll(high, 16 * bit, 1), low)
                group[m | bit] = jnp.where(up, high, pltpu.roll(low, 128 - 16 * bit, 1))
        for i in range(8 if tile < 9 else 4):
            out_ref[:, 0, pl.ds((tile * 8 + i) * 128, 128)] = group[i]


def restore_kernel(in_ref, out_ref):
    for first in range(0, LEVELS, 19):
        tiles = [in_ref[:, 0, pl.ds((first + i) * 128, 128)] for i in range(19)]
        for i, moved in enumerate(swap_blocks(tiles)):
            out_ref[first + i] = moved


def params():
    return pltpu.CompilerParams(vmem_limit_bytes=VMEM_LIMIT)


def deal(cells):
    return pl.pallas_call(
        deal_kernel,
        out_shape=jax.ShapeDtypeStruct((4, LEVELS, 2, 4 * GY), F32),
        compiler_params=params(),
        name="deal",
    )(cells)


def forecast_interior(main, mixing, rate, operator):
    return pl.pallas_call(
        interior_kernel,
        out_shape=[
            jax.ShapeDtypeStruct((64, 1, PAIR), F32),
            jax.ShapeDtypeStruct((NSTEP - 1, 2, 4, PADDED, GY), F32),
            jax.ShapeDtypeStruct((PADDED, 3 * PADDED), BF16),
            jax.ShapeDtypeStruct((PADDED, GY), F32),
            jax.ShapeDtypeStruct((2 * 128, LANES), F32),
        ],
        scratch_shapes=[pltpu.VMEM((2, 2, 16, PADDED, GY), F32)],
        compiler_params=params(),
        cost_estimate=pl.CostEstimate(flops=10**10, bytes_accessed=8 * 2**20, transcendentals=0),
        name="interior",
    )(main, mixing, rate, operator)


def forecast_edges(main, before, after, inner, edges, mixing, rate):
    return pl.pallas_call(
        edge_kernel,
        out_shape=jax.ShapeDtypeStruct((128, 1, PAIR), F32),
        scratch_shapes=[pltpu.VMEM((2, 2, 2, 6, PADDED, GY), F32), pltpu.SemaphoreType.DMA],
        compiler_params=params(),
        name="edges",
    )(main, after, before, inner, edges, mixing, rate)


def analyse(cells, operator, observed, precisions):
    return pl.pallas_call(
        analysis_kernel,
        out_shape=jax.ShapeDtypeStruct((32, 1, 4 * PAIR), F32),
        scratch_shapes=[
            pltpu.VMEM((MEMBERS + 8, LANES), F32),
            pltpu.VMEM((MEMBERS + 8, 2 * 128), F32),
            pltpu.VMEM((MEMBERS, LANES), F32),
            pltpu.VMEM((2, 2, MEMBERS, MEMBERS), BF16),
            *([pltpu.VMEM((MEMBERS, MEMBERS), BF16)] * 18),
        ],
        compiler_params=params(),
        name="analysis",
    )(cells, operator, observed, precisions)


def restore(cells):
    return pl.pallas_call(
        restore_kernel,
        grid=(4,),
        in_specs=[pl.BlockSpec((8, 1, 4 * PAIR), lambda y: (y, 0, 0))],
        out_specs=pl.BlockSpec((LEVELS, 8, GY), lambda y: (0, 0, y)),
        out_shape=jax.ShapeDtypeStruct((LEVELS, 8, 4 * GY), F32),
        compiler_params=params(),
        name="restore",
    )(cells)


def prepare(blending_matrix, lateral_spreading):
    extra = PADDED - LEVELS
    mixing = jnp.tile(jnp.pad(blending_matrix, ((0, extra), (0, extra))), (1, 3))
    return mixing, jnp.pad(lateral_spreading, (0, extra))[:, None]


def shards(ensemble, blending_matrix, lateral_spreading, obs_op, obs_value, obs_precision):
    mixing, rate = prepare(blending_matrix, lateral_spreading)
    split = deal(ensemble.transpose(1, 0, 2))
    main = lax.all_to_all(split, "x", split_axis=0, concat_axis=0, tiled=True)
    after = lax.ppermute(main[0], "zh", [((i + 1) % 4, i) for i in range(4)])
    before = lax.ppermute(main[3], "zh", [(i, (i + 1) % 4) for i in range(4)])
    inner, edges, mixed, rates, wide = forecast_interior(main, mixing, rate, obs_op)
    sent = forecast_edges(main, before, after, inner, edges, mixed, rates)
    owned = lax.all_to_all(sent, ("x", "y", "zl", "c"), split_axis=0, concat_axis=0, tiled=True)
    result = analyse(owned, wide, obs_value, obs_precision)
    returned = lax.all_to_all(result, ("y", "zl", "c"), split_axis=0, concat_axis=0, tiled=True)
    return restore(returned).transpose(1, 0, 2)


def solution(mesh):
    fine = Mesh(mesh.devices.reshape(4, 4, 2, 4, 4), ("y", "zl", "c", "zh", "x"))
    member, region = ("y", "zl", "c"), ("zh", "x")
    return jax.shard_map(
        shards,
        mesh=fine,
        in_specs=(
            P(member, None, region),
            P(),
            P(),
            P(region + member, None, None),
            P(region + member, None),
            P(region + member, None),
        ),
        out_specs=P(member, None, region),
        check_vma=False,
    )
```

```python
import math

import jax
import jax.numpy as jnp
from jax import lax
from jax.experimental import pallas as pl
from jax.experimental.pallas import tpu as pltpu
from jax.sharding import Mesh, PartitionSpec as P

F32 = jnp.float32
BF16 = jnp.bfloat16
HIGHEST = lax.Precision.HIGHEST
LEVELS = 76
PADDED = 80
GY = 128
NSTEP = 4
ITERS = 12
MEMBERS = 256
PAIR = 2 * LEVELS * 16
TILES = PAIR // 128
HALF = LEVELS * 16
LANES = 1280
VMEM_LIMIT = 32 * 1024 * 1024


def lane_index(shape):
    return lax.broadcasted_iota(jnp.int32, shape, len(shape) - 1)


def split3(x):
    high = x.astype(BF16)
    rest = x - high.astype(F32)
    mid = rest.astype(BF16)
    low = (rest - mid.astype(F32)).astype(BF16)
    return high, mid, low


def swap_blocks(tiles):
    sub = lax.broadcasted_iota(jnp.int32, (8, 128), 0)
    lane = lane_index((8, 128))
    block, col = lane // 16, lane % 16
    skew = ((block + sub) % 8) * 16 + col
    turn = (sub - block) % 8
    back = turn * 16 + col
    result = []
    for x in tiles:
        for index, axis in ((skew, 1), (turn, 0), (back, 1)):
            x = jnp.take_along_axis(x, index, axis=axis, mode="promise_in_bounds")
        result.append(x)
    return result


def advance(window, mix_ref, rate_ref):
    centre = window[1:3]
    high, mid, _ = split3(jnp.concatenate(centre, axis=1))
    stacked = jnp.concatenate([high, mid, high], axis=0)
    coupled = jnp.dot(mix_ref[...], stacked, preferred_element_type=F32)
    result = []
    for i in range(2):
        cells = centre[i]
        around = window[i] + window[i + 2]
        laplace = around + pltpu.roll(cells, GY - 1, 1) + pltpu.roll(cells, 1, 1) - 4.0 * cells
        pushed = jnp.tanh(coupled[:, i * GY : (i + 1) * GY])
        result.append(cells + rate_ref[...] * laplace + 0.3 * pushed)
    return result


def send_rows(results, row, out_ref):
    for i in range(2):
        both = jnp.concatenate([results[m][i][0:LEVELS] for m in range(2)], axis=0)
        moved = swap_blocks([both[tile * 8 : tile * 8 + 8] for tile in range(TILES)])
        for tile in range(TILES):
            out_ref[pl.ds((row + i) * 8, 8), 0, pl.ds(tile * 128, 128)] = moved[tile]


def put_row(state_ref, index, cells):
    state_ref[index + (slice(0, LEVELS), slice(None))] = cells
    state_ref[index + (slice(LEVELS, PADDED), slice(None))] = jnp.zeros((PADDED - LEVELS, GY), F32)


def deal_kernel(in_ref, out_ref):
    for x in range(4):
        out_ref[x] = in_ref[:, 2 * x : 2 * x + 2, :]


def interior_kernel(main_ref, mix_ref, rate_ref, op_ref, out_ref, edge_ref, mix_out, rate_out, wide_ref, state):
    table = mix_ref[...]
    high, mid, _ = split3(table)
    part = lane_index(table.shape) // PADDED
    mix_out[...] = jnp.where(part == 2, mid.astype(F32), high.astype(F32)).astype(BF16)
    rate_out[...] = jnp.broadcast_to(rate_ref[...], (PADDED, GY))
    for m in range(2):
        for row in range(16):
            put_row(state, (0, m, row), main_ref[row // 4, :, m, pl.ds((row % 4) * GY, GY)])
    for step in range(NSTEP):
        now = step % 2

        def body(pair, carry, now=now, step=step):
            row = step + 1 + 2 * pair
            results = [
                advance([state[now, m, row - 1 + i] for i in range(4)], mix_out, rate_out)
                for m in range(2)
            ]
            if step < NSTEP - 1:
                for m in range(2):
                    for i in range(2):
                        state[1 - now, m, row + i] = results[m][i]
            else:
                send_rows(results, row - 4, out_ref)
            return carry

        lax.fori_loop(0, (14 - 2 * step) // 2, body, 0)
        if step < NSTEP - 1:
            done = step + 1
            for m in range(2):
                for i, row in enumerate((done, done + 1, 14 - done, 15 - done)):
                    edge_ref[step, m, i] = state[1 - now, m, row]

    take = lax.broadcasted_iota(jnp.int32, (128, 256), 0)
    put = lane_index((128, 256))
    same = (put // 16 == take // 8) & (put % 8 == take % 8)
    spread = jnp.where(same, 1.0, 0.0).astype(BF16)
    group = (lane_index((128, 256)) // 8) % 2
    for j in range(2):
        for block in range(5):
            width = 128 if block < 4 else 608 - 512
            piece = split3(op_ref[j, :, pl.ds(block * 128, width)])
            grown = [jnp.dot(p, spread[0:width], preferred_element_type=F32) for p in piece]
            for i in range(3):
                wide_ref[i, j * 128 : (j + 1) * 128, block * 256 : (block + 1) * 256] = jnp.where(
                    group == j, grown[i], 0.0
                ).astype(BF16)


def edge_kernel(main_ref, next_ref, prev_ref, inner_ref, edge_ref, mix_ref, rate_ref, out_ref, state, sem):
    inner = pltpu.make_async_copy(inner_ref, out_ref.at[pl.ds(32, 64)], sem)
    inner.start()
    for m in range(2):
        for i in range(4):
            cols = pl.ds(i * GY, GY)
            put_row(state, (0, 0, m, i), prev_ref[:, m, cols])
            put_row(state, (0, 1, m, 2 + i), next_ref[:, m, cols])
        for i in range(2):
            put_row(state, (0, 0, m, 4 + i), main_ref[0, :, m, pl.ds(i * GY, GY)])
            put_row(state, (0, 1, m, i), main_ref[3, :, m, pl.ds((2 + i) * GY, GY)])
    for step in range(NSTEP):
        now = step % 2

        def body(index, carry, now=now, step=step):
            side, pair = index // 2, index % 2
            results = [
                advance([state[now, side, m, 2 * pair + i] for i in range(4)], mix_ref, rate_ref)
                for m in range(2)
            ]
            if step < NSTEP - 1:
                for m in range(2):
                    for i in range(2):
                        state[1 - now, side, m, 2 * side + 2 * pair + i] = results[m][i]
            else:
                send_rows(results, 12 * side + 2 * pair, out_ref)
            return carry

        lax.fori_loop(0, 4, body, 0)
        if step < NSTEP - 1:
            for m in range(2):
                for i in range(2):
                    state[1 - now, 0, m, 4 + i] = edge_ref[step, m, i]
                    state[1 - now, 1, m, i] = edge_ref[step, m, 2 + i]

    inner.wait()


def analysis_kernel(x_ref, wide, obs_ref, prec_ref, out_ref, pert, yref, moved, roots, *parts):
    low_half = lane_index((128, 128)) < 64
    rows = 128
    for tile in range(10):
        even = x_ref[:, 0, pl.ds(tile * 128, 128)]
        first = x_ref[:, 0, pl.ds((9 + tile) * 128, 128)]
        if tile < 9:
            second = x_ref[:, 0, pl.ds((10 + tile) * 128, 128)]
            odd = pltpu.roll(jnp.where(low_half, second, first), 64, 1)
        else:
            even = jnp.where(low_half, even, 0.0)
            odd = jnp.where(low_half, pltpu.roll(first, 64, 1), 0.0)
        mean = (jnp.sum(even, axis=0, keepdims=True) + jnp.sum(odd, axis=0, keepdims=True)) / MEMBERS
        lanes = pl.ds(tile * 128, 128)
        pert[0:rows, lanes] = even - mean
        pert[rows : 2 * rows, lanes] = odd - mean
        pert[2 * rows : 2 * rows + 16, lanes] = jnp.broadcast_to(mean, (16, 128))

    pieces = split3(pert[...])
    sums = None
    for i, k in ((2, 0), (0, 2), (1, 1), (1, 0), (0, 1), (0, 0)):
        term = lax.dot_general(
            pieces[i], wide[k], (((1,), (1,)), ((), ())), preferred_element_type=F32
        )
        sums = term if sums is None else term + sums
    yref[...] = sums
    eye = jnp.where(
        lax.broadcasted_iota(jnp.int32, (MEMBERS, MEMBERS), 0) == lane_index((MEMBERS, MEMBERS)), 1.0, 0.0
    )

    def mm(a, b):
        return jnp.dot(a, b, precision=HIGHEST, preferred_element_type=F32)

    def put(refs, x):
        for ref, part in zip(refs, split3(x)):
            ref[...] = part

    def product(a, b):
        total = None
        for i, k in ((2, 0), (0, 2), (1, 1), (1, 0), (0, 1), (0, 0)):
            term = jnp.dot(a[i][...], b[k][...], preferred_element_type=F32)
            total = term if total is None else term + total
        return total

    rr, zz, ff = [[parts[9 * j + 3 * i : 9 * j + 3 * i + 3] for j in range(2)] for i in range(3)]
    scale = []
    for j in range(2):
        obs = slice(j * 128, (j + 1) * 128)
        y = yref[0:MEMBERS, obs]
        weighted = y * prec_ref[j : j + 1, :]
        gram = lax.dot_general(
            weighted, y, (((1,), (1,)), ((), ())), precision=HIGHEST, preferred_element_type=F32
        )
        system = (MEMBERS - 1.0) * eye + gram
        norm = jnp.sqrt(jnp.sum(jnp.sum(system * system, axis=0, keepdims=True), axis=1, keepdims=True))
        scale.append(norm)
        start = system / norm
        factor = 0.5 * (3.0 * eye - start)
        put(zz[j], factor)
        put(rr[j], mm(start, factor))

    def newton(last=False):
        for j in range(2):
            put(ff[j], 0.5 * (3.0 * eye - product(zz[j], rr[j])))
        if last:
            return [product(ff[j], zz[j]) for j in range(2)]
        for j in range(2):
            put(rr[j], product(rr[j], ff[j]))
        for j in range(2):
            put(zz[j], product(ff[j], zz[j]))
        return None

    def body(step, carry):
        newton()
        return carry

    lax.fori_loop(0, ITERS - 2, body, 0)
    ends = newton(last=True)
    shifts = []
    for j in range(2):
        root = ends[j] / jnp.sqrt(scale[j])
        obs = slice(j * 128, (j + 1) * 128)
        y = yref[0:MEMBERS, obs]
        innovation = obs_ref[j : j + 1, :] - yref[MEMBERS : MEMBERS + 1, obs]
        pull = jnp.sum(y * prec_ref[j : j + 1, :] * innovation, axis=1, keepdims=True)
        half = jnp.sum(root * pull, axis=0, keepdims=True)
        weight = jnp.sum(root * half, axis=1, keepdims=True)
        shifts.append(weight)
        for i, part in enumerate(split3(math.sqrt(MEMBERS - 1.0) * root)[0:2]):
            roots[i, j] = part
    for block in range(5):
        lanes = pl.ds(block * 256, 256)
        own = (lane_index((MEMBERS, 256)) // 8) % 2 == 0
        cells = pert[0:MEMBERS, lanes]
        high, mid, _ = split3(cells)
        terms = []
        for j in range(2):
            base = pert[MEMBERS : MEMBERS + 1, lanes] + jnp.sum(cells * shifts[j], axis=0, keepdims=True)
            small = jnp.dot(roots[0, j], mid, preferred_element_type=F32) + jnp.dot(
                roots[1, j], high, preferred_element_type=F32
            )
            terms.append(base + (jnp.dot(roots[0, j], high, preferred_element_type=F32) + small))
        moved[:, lanes] = jnp.where(own, terms[0], terms[1])
    lane_block = lane_index((32, 128)) // 16
    for tile in range(10):
        cols = pl.ds(tile * 128, 128)
        group = [moved[(m % 2) * rows + (m // 2) * 32 : (m % 2) * rows + (m // 2) * 32 + 32, cols] for m in range(8)]
        for bit in (1, 2, 4):
            up = (lane_block & bit) != 0
            for m in range(8):
                if m & bit:
                    continue
                low, high = group[m], group[m | bit]
                group[m] = jnp.where(up, pltpu.roll(high, 16 * bit, 1), low)
                group[m | bit] = jnp.where(up, high, pltpu.roll(low, 128 - 16 * bit, 1))
        for i in range(8 if tile < 9 else 4):
            out_ref[:, 0, pl.ds((tile * 8 + i) * 128, 128)] = group[i]


def restore_kernel(in_ref, out_ref):
    for first in range(0, LEVELS, 19):
        tiles = [in_ref[:, 0, pl.ds((first + i) * 128, 128)] for i in range(19)]
        for i, moved in enumerate(swap_blocks(tiles)):
            out_ref[first + i] = moved


def params():
    return pltpu.CompilerParams(vmem_limit_bytes=VMEM_LIMIT)


def deal(cells):
    return pl.pallas_call(
        deal_kernel,
        out_shape=jax.ShapeDtypeStruct((4, LEVELS, 2, 4 * GY), F32),
        compiler_params=params(),
        name="deal",
    )(cells)


def forecast_interior(main, mixing, rate, operator):
    return pl.pallas_call(
        interior_kernel,
        out_shape=[
            jax.ShapeDtypeStruct((64, 1, PAIR), F32),
            jax.ShapeDtypeStruct((NSTEP - 1, 2, 4, PADDED, GY), F32),
            jax.ShapeDtypeStruct((PADDED, 3 * PADDED), BF16),
            jax.ShapeDtypeStruct((PADDED, GY), F32),
            jax.ShapeDtypeStruct((3, 2 * 128, LANES), BF16),
        ],
        scratch_shapes=[pltpu.VMEM((2, 2, 16, PADDED, GY), F32)],
        compiler_params=params(),
        cost_estimate=pl.CostEstimate(flops=10**10, bytes_accessed=8 * 2**20, transcendentals=0),
        name="interior",
    )(main, mixing, rate, operator)


def forecast_edges(main, before, after, inner, edges, mixing, rate):
    return pl.pallas_call(
        edge_kernel,
        out_shape=jax.ShapeDtypeStruct((128, 1, PAIR), F32),
        scratch_shapes=[pltpu.VMEM((2, 2, 2, 6, PADDED, GY), F32), pltpu.SemaphoreType.DMA],
        compiler_params=params(),
        name="edges",
    )(main, after, before, inner, edges, mixing, rate)


def analyse(cells, operator, observed, precisions):
    return pl.pallas_call(
        analysis_kernel,
        out_shape=jax.ShapeDtypeStruct((32, 1, 4 * PAIR), F32),
        scratch_shapes=[
            pltpu.VMEM((MEMBERS + 16, LANES), F32),
            pltpu.VMEM((MEMBERS + 16, 2 * 128), F32),
            pltpu.VMEM((MEMBERS, LANES), F32),
            pltpu.VMEM((2, 2, MEMBERS, MEMBERS), BF16),
            *([pltpu.VMEM((MEMBERS, MEMBERS), BF16)] * 18),
        ],
        compiler_params=params(),
        name="analysis",
    )(cells, operator, observed, precisions)


def restore(cells):
    return pl.pallas_call(
        restore_kernel,
        grid=(4,),
        in_specs=[pl.BlockSpec((8, 1, 4 * PAIR), lambda y: (y, 0, 0))],
        out_specs=pl.BlockSpec((LEVELS, 8, GY), lambda y: (0, 0, y)),
        out_shape=jax.ShapeDtypeStruct((LEVELS, 8, 4 * GY), F32),
        compiler_params=params(),
        name="restore",
    )(cells)


def prepare(blending_matrix, lateral_spreading):
    extra = PADDED - LEVELS
    mixing = jnp.tile(jnp.pad(blending_matrix, ((0, extra), (0, extra))), (1, 3))
    return mixing, jnp.pad(lateral_spreading, (0, extra))[:, None]


def shards(ensemble, blending_matrix, lateral_spreading, obs_op, obs_value, obs_precision):
    mixing, rate = prepare(blending_matrix, lateral_spreading)
    split = deal(ensemble.transpose(1, 0, 2))
    main = lax.all_to_all(split, "x", split_axis=0, concat_axis=0, tiled=True)
    after = lax.ppermute(main[0], "zh", [((i + 1) % 4, i) for i in range(4)])
    before = lax.ppermute(main[3], "zh", [(i, (i + 1) % 4) for i in range(4)])
    inner, edges, mixed, rates, wide = forecast_interior(main, mixing, rate, obs_op)
    sent = forecast_edges(main, before, after, inner, edges, mixed, rates)
    owned = lax.all_to_all(sent, ("x", "y", "zl", "c"), split_axis=0, concat_axis=0, tiled=True)
    result = analyse(owned, wide, obs_value, obs_precision)
    returned = lax.all_to_all(result, ("y", "zl", "c"), split_axis=0, concat_axis=0, tiled=True)
    return restore(returned).transpose(1, 0, 2)


def solution(mesh):
    fine = Mesh(mesh.devices.reshape(4, 4, 2, 4, 4), ("y", "zl", "c", "zh", "x"))
    member, region = ("y", "zl", "c"), ("zh", "x")
    return jax.shard_map(
        shards,
        mesh=fine,
        in_specs=(
            P(member, None, region),
            P(),
            P(),
            P(region + member, None, None),
            P(region + member, None),
            P(region + member, None),
        ),
        out_specs=P(member, None, region),
        check_vma=False,
    )
```
